128 devices in a mesh: tile: 32 (over x, y_hi, z), tm: 4 (over y_lo, core).
Axes of the slice: x: 4, y: 4 (y_hi: 2, y_lo: 2; y = y_hi * 2 + y_lo), z: 4, core: 2. Of those that a mesh axis runs over, the one named last changes fastest.
Arguments:
- volume: bfloat16 [16, 256, 16, 128], P('tm', 'tile'), may hold values from -6 to 6
- frame_index: int32 [16], P('tm'), may hold values from 0 to 31, as said below
- tile_offset: int32 [3], replicated, may hold values from 0 to 255
- conv_first: bfloat16 [16, 1, 3, 3, 3], replicated, may hold values from -1.25 to 1.25
- conv_second: bfloat16 [16, 16, 3, 3, 3], replicated, may hold values from -0.3125 to 0.3125
- patch_weight: bfloat16 [8192, 1024], replicated, may hold values from -0.5 to 0.5
- attend_weight: bfloat16 [1024, 3072], P(None, 'tile')
- mixing_weight: bfloat16 [1024, 1024], P(None, 'tile'), may hold values from -0.1875 to 0.1875
- cube_output_projector: bfloat16 [1024, 512], replicated, may hold values from -0.1875 to 0.1875
Outputs:
- prediction_tensor: bfloat16 [16, 32, 2, 16, 512], P('tm', 'tile')
The draws below stay inside these ranges and needn't reach their ends.
Inputs may be any that keep to these rules, and one draw needn't show every extreme that they name: `frame_index`: strictly increasing; the first frame is 0 and the last is 31.
All inputs are finite; a program needn't handle non-finite values.
Results may differ from the reference program's by a relative error of at most 0.015.
Values may be sent and summed in bfloat16 or wider, within the bound.
No kernel may reach another device: no remote copies, remote signals or barrier semaphores. Data moves between devices by JAX's collectives and lax.ppermute only.
A program may use at most 256 MiB of HBM per device.

```python
import math
import jax
import jax.numpy as jnp
from jax import lax

CH = 16
D = 1024
HEADS = 8
HD = 128
BLOCK_EDGE_UNITS = 8
PRIOR_SNAPSHOTS = 16
UNITS_DOWNWARD = 16
UNITS_LENGTHWAYS = 128
UNITS_WIDEWAYS = 256
PV = 512
N_TILE = 32


def draw_frame_index(key, part):
    chosen = jax.random.permutation(key, 2 * PRIOR_SNAPSHOTS - 2) + 1
    middle = jnp.sort(chosen[:PRIOR_SNAPSHOTS - 2]).astype(jnp.int32)
    return jnp.concatenate([jnp.zeros((1,), jnp.int32), middle, jnp.full((1,), 2 * PRIOR_SNAPSHOTS - 1, jnp.int32)])


def draw_attend_weight(key, part):
    matrix = jax.random.normal(key, (D, 3 * D), jnp.float32) * D ** (-0.5)
    return matrix.astype(jnp.bfloat16)


def block_scale(rng, dims, pieces, least, high):
    loudness, own = 1.0, jax.random.fold_in(rng, 6)
    for position, shards_of in pieces:
        heights = jnp.exp(jax.random.uniform(jax.random.fold_in(own, position), (shards_of,), jnp.float32, least / len(pieces), high / len(pieces)))
        loudness = loudness * jnp.repeat(heights, dims[position] // shards_of).reshape([-1 if axis == position else 1 for axis in range(len(dims))])
    return loudness


def scatter_about(stream_key, dims, spread, reach, split=(), kind=jnp.bfloat16):
    array = spread * jax.random.normal(stream_key, dims, jnp.float32)
    if split:
        array = array * block_scale(stream_key, dims, split, -0.22, 0.18)
    return jnp.clip(array, -reach, reach).astype(kind)


def setup_inputs(seed: int = 0) -> dict:
    key_of = jax.random.split(jax.random.key(seed), 10)
    return {
        "volume": scatter_about(key_of[0], (PRIOR_SNAPSHOTS, UNITS_WIDEWAYS, UNITS_DOWNWARD, UNITS_LENGTHWAYS), 1.0, 6.0, ((0, 4), (1, 32))),
        "frame_index": draw_frame_index(jax.random.fold_in(key_of[9], 71), 0),
        "tile_offset": jax.random.randint(key_of[2], (3,), 0, 256).astype(jnp.int32),
        "conv_first": scatter_about(key_of[3], (CH, 1, 3, 3, 3), 27 ** -0.5, 1.25),
        "conv_second": scatter_about(key_of[4], (CH, CH, 3, 3, 3), (27 * CH) ** -0.5, 0.3125),
        "patch_weight": scatter_about(key_of[5], (CH * PV, D), (CH * PV // 64) ** -0.5, 0.5),
        "attend_weight": draw_attend_weight(jax.random.fold_in(key_of[9], 71), 0),
        "mixing_weight": scatter_about(key_of[7], (D, D), D ** -0.5, 0.1875, ((1, 32),)),
        "cube_output_projector": scatter_about(key_of[8], (D, PV), D ** -0.5, 0.1875),
    }


def convolve(field_in, kernel):
    return lax.conv_general_dilated(field_in, kernel, (1, 1, 1), ((1, 1), (1, 1), (1, 1)), dimension_numbers=('NCDHW', 'OIDHW', 'NCDHW'), preferred_element_type=jnp.float32)

def settle(values_in):
    return values_in * lax.rsqrt(lax.optimization_barrier(jnp.mean(values_in * values_in, axis=-1, keepdims=True)) + 1e-05)

def embed_time(frame_index):
    frequency = jnp.exp(-math.log(1000.0) * jnp.arange(D, dtype=jnp.float32) / D)
    phase_shift = (jnp.arange(D) % 2).astype(jnp.float32) * (math.pi / 2)
    return (jnp.sin(frame_index.astype(jnp.float32)[:, None] * frequency + phase_shift), frequency)

def embed_space(tile_offset, place_x, place_z, place_y, frequency):
    along_x = (tile_offset[0] + BLOCK_EDGE_UNITS * place_x).astype(jnp.float32)
    along_z = (tile_offset[1] + BLOCK_EDGE_UNITS * place_z).astype(jnp.float32)
    along_y = (tile_offset[2] + BLOCK_EDGE_UNITS * place_y).astype(jnp.float32)
    summed = jnp.sin(along_x[:, None, None, None] * frequency) + jnp.sin(along_z[None, :, None, None] * frequency + 1.0)
    summed = summed + jnp.sin(along_y[None, None, :, None] * frequency + 2.0)
    return summed.reshape(-1, D)

def attend_frames(query, keys_all, values_all, first_frame):
    cube_count = keys_all.shape[1]
    scores = jnp.einsum('tnhd,smhd->htnsm', query.astype(jnp.float32), keys_all.astype(jnp.float32)) / math.sqrt(HD)
    scores = scores.reshape(scores.shape[0], query.shape[0], query.shape[1], -1)
    query_frame = first_frame + jnp.arange(query.shape[0])
    allowed = jnp.arange(keys_all.shape[0])[None, :] <= query_frame[:, None]
    allowed = jnp.repeat(allowed, cube_count, axis=1)
    scores = jnp.where(allowed[None, :, None, :], scores, -1e+30)
    shifted = jnp.exp(scores - lax.optimization_barrier(jnp.max(scores, axis=-1, keepdims=True)))
    weights = (shifted / lax.optimization_barrier(jnp.sum(shifted, axis=-1, keepdims=True))).astype(jnp.bfloat16)
    flat_values = values_all.reshape(-1, values_all.shape[2], values_all.shape[3])
    return jnp.einsum('htnk,khd->tnhd', weights.astype(jnp.float32), flat_values.astype(jnp.float32)).astype(jnp.bfloat16)

def reference(volume, frame_index, tile_offset, conv_first, conv_second, patch_weight, attend_weight, mixing_weight, cube_output_projector):

    def encode(frame_cells):
        first_maps = jax.nn.silu(convolve(frame_cells[None, None], conv_first)).astype(jnp.bfloat16)
        second_maps = jax.nn.silu(convolve(first_maps, conv_second)).astype(jnp.bfloat16)[0]
        patch_cubes = second_maps.reshape(CH, UNITS_WIDEWAYS // BLOCK_EDGE_UNITS, BLOCK_EDGE_UNITS, UNITS_DOWNWARD // BLOCK_EDGE_UNITS, BLOCK_EDGE_UNITS, UNITS_LENGTHWAYS // BLOCK_EDGE_UNITS, BLOCK_EDGE_UNITS)
        patch_cubes = patch_cubes.transpose(1, 3, 5, 0, 2, 4, 6).reshape(-1, CH * BLOCK_EDGE_UNITS ** 3)
        return jnp.dot(patch_cubes, patch_weight, preferred_element_type=jnp.float32)
    encoded = lax.map(encode, volume)
    time_emb, frequency = embed_time(frame_index)
    space_emb = embed_space(tile_offset, jnp.arange(UNITS_WIDEWAYS // BLOCK_EDGE_UNITS), jnp.arange(UNITS_DOWNWARD // BLOCK_EDGE_UNITS), jnp.arange(UNITS_LENGTHWAYS // BLOCK_EDGE_UNITS), frequency)
    tokens = (encoded + time_emb[:, None, :] + space_emb[None]).astype(jnp.bfloat16)
    token_rows = tokens.reshape(-1, D)
    normed = settle(token_rows.astype(jnp.float32)).astype(jnp.bfloat16)
    projected = jnp.dot(normed, attend_weight, preferred_element_type=jnp.float32).astype(jnp.bfloat16)
    projected = projected.reshape(PRIOR_SNAPSHOTS, N_TILE, -1, 3, HEADS, HD).transpose(1, 0, 2, 3, 4, 5)

    def strip_attend(strip_rows):
        return attend_frames(strip_rows[:, :, 0], strip_rows[:, :, 1], strip_rows[:, :, 2], 0)
    attended = lax.map(strip_attend, projected).transpose(1, 0, 2, 3, 4)
    residual = token_rows.astype(jnp.float32) + jnp.dot(attended.reshape(-1, D), mixing_weight, preferred_element_type=jnp.float32)
    ending_entries = settle(residual).astype(jnp.bfloat16)
    prediction_tensor = jnp.dot(ending_entries, cube_output_projector, preferred_element_type=jnp.float32).astype(jnp.bfloat16)
    return prediction_tensor.reshape(PRIOR_SNAPSHOTS, UNITS_WIDEWAYS // BLOCK_EDGE_UNITS, UNITS_DOWNWARD // BLOCK_EDGE_UNITS, UNITS_LENGTHWAYS // BLOCK_EDGE_UNITS, BLOCK_EDGE_UNITS ** 3)
```

```python
import functools
import math

import jax
import jax.numpy as jnp
from jax import lax
from jax.experimental import pallas as pl
from jax.experimental.pallas import tpu as pltpu
from jax.sharding import PartitionSpec as P

CH = 16
D = 1024
HEADS = 8
HD = 128
BLOCK_EDGE_UNITS = 8

F32 = jnp.float32
BF16 = jnp.bfloat16

ROWS = 8
XV = 12
XM = 10
ZV = 12
ZM = 10
BLK = 128
PAIRS = 8


def silu(v):
    return 0.5 * v * (1.0 + jnp.tanh(0.5 * v))


def weights_kernel(first_ref, second_ref, g_ref, w2_ref):
    col = lax.broadcasted_iota(jnp.int32, (48, 768), 1)
    row = lax.broadcasted_iota(jnp.int32, (48, 768), 0)
    spread = (
        ((col // 256) == (row // CH)) & (((col % 128) // 8) == (row % CH))
    ).astype(BF16)
    first = jnp.dot(first_ref[...], spread, preferred_element_type=F32)
    second = jnp.dot(second_ref[...], spread, preferred_element_type=F32).astype(BF16)

    lane = lax.broadcasted_iota(jnp.int32, (48, 256), 1)
    here = lax.broadcasted_iota(jnp.int32, (48, 256), 0) - 16
    out_y = (lane // 128) * 8 + lane % 8
    for tap in range(9):
        total = jnp.zeros((48, 256), F32)
        for k in range(3):
            value = first[tap : tap + 1, 256 * k : 256 * (k + 1)]
            total = total + jnp.where(here == out_y + (k - 1), value, 0.0)
        g_ref[tap] = total.astype(BF16)

    r = lax.broadcasted_iota(jnp.int32, (512, CH), 0)
    c = lax.broadcasted_iota(jnp.int32, (512, CH), 1)
    pick = (((r % 128) // 8) == c).astype(BF16)
    lane = lax.broadcasted_iota(jnp.int32, (512, 256), 1)
    r = lax.broadcasted_iota(jnp.int32, (512, 256), 0)
    shift = (r // 128 - 1) * 8 + r % 8 - ((lane // 128) * 8 + lane % 8)
    for tap in range(9):
        rows = jnp.dot(
            pick, second[CH * tap : CH * (tap + 1)], preferred_element_type=F32
        )
        total = jnp.zeros((512, 256), F32)
        for k in range(3):
            total = total + jnp.where(
                shift == k - 1, rows[:, 256 * k : 256 * (k + 1)], 0.0
            )
        w2_ref[tap] = total.astype(BF16)


def encode_kernel(
    place_ref,
    volume_ref,
    left_ref,
    right_ref,
    g_ref,
    w2_ref,
    time_ref,
    space_ref,
    along_y_ref,
    patch_hbm,
    tokens_ref,
    normed_ref,
    cells,
    planes,
    taps,
    w1,
    maps_even,
    maps_odd,
    second,
    patch,
    patch_sem,
):
    copies = [
        pltpu.make_async_copy(
            patch_hbm.at[:, pl.ds(8 * i, 8)],
            patch.at[:, pl.ds(8 * i, 8)],
            patch_sem.at[i],
        )
        for i in range(8)
    ]
    for copy in copies:
        copy.start()
    place = place_ref[0]
    count = place_ref[1]

    cells[:, 0:2] = left_ref[...].astype(F32)
    cells[:, 2:10] = volume_ref[...].astype(F32)
    cells[:, 10:12] = right_ref[...].astype(F32)
    planes[...] = jnp.zeros_like(planes)
    for x in range(XV):
        for f in range(4):
            planes[x, pl.ds(16 + 2 * f, 10, stride=8), :] = cells[f, x, pl.ds(0, 10), :]
            planes[x, pl.ds(2 * f + 1, 10, stride=8), :] = cells[f, x, pl.ds(6, 10), :]
    for dx in range(3):
        for dz in range(3):
            tap = 3 * dx + dz
            for x in range(XM):
                taps[x, :, BLK * tap : BLK * (tap + 1)] = planes[
                    x + dx, 8 * dz : 8 * dz + 80, :
                ].astype(BF16)

    w1[...] = jnp.zeros_like(w1)
    maps_even[:, :, 0:BLK] = jnp.zeros((XM, 80, BLK), BF16)
    maps_even[:, :, 17 * BLK :] = jnp.zeros((XM, 80, BLK), BF16)
    maps_odd[:, :, 0:BLK] = jnp.zeros((XM, 64, BLK), BF16)
    maps_odd[:, :, 17 * BLK :] = jnp.zeros((XM, 64, BLK), BF16)

    x = lax.broadcasted_iota(jnp.int32, (XM, 80, 1), 0) + 8 * place - 1
    r = lax.broadcasted_iota(jnp.int32, (XM, 80, 1), 1)
    z = 8 * (r % 2) + r // 8 - 1
    inside = (x >= 0) & (x < 8 * count) & (z >= 0) & (z < 16)

    def first_step(n, carry):
        before = pl.ds(pl.multiple_of(16 * jnp.maximum(n - 1, 0), 16), 16)
        now = pl.ds(pl.multiple_of(16 * n, 16), 48)
        for tap in range(9):
            w1[tap, before, :] = jnp.zeros((16, 256), BF16)
            w1[tap, now, :] = g_ref[tap]
        acc = jnp.zeros((XM * 80, 256), F32)
        for tap in range(9):
            acc = acc + jnp.dot(
                taps[:, :, BLK * tap : BLK * (tap + 1)].reshape(XM * 80, BLK),
                w1[tap, 16:144, :],
                preferred_element_type=F32,
            )
        out = jnp.where(inside, silu(acc).reshape(XM, 80, 256), 0.0)
        lanes = pl.ds(pl.multiple_of(256 * n + BLK, BLK), 256)
        maps_even[:, :, lanes] = out.astype(BF16)
        maps_odd[:, :, lanes] = out[:, 8:72].astype(BF16)
        return carry

    lax.fori_loop(0, PAIRS, first_step, 0)

    def second_step(p, carry):
        lanes = pl.ds(pl.multiple_of(256 * p, 256), 512)
        acc = jnp.zeros((512, 256), F32)
        for dx in range(3):
            for dz in range(3):
                if dz == 1:
                    source = maps_odd[dx : dx + 8, :, lanes]
                else:
                    source = maps_even[dx : dx + 8, 8 * dz : 8 * dz + 64, lanes]
                acc = acc + jnp.dot(
                    source.reshape(512, 512), w2_ref[3 * dx + dz], preferred_element_type=F32
                )
        out = silu(acc)
        both = jnp.concatenate(
            [out[:, :BLK].reshape(64, 8, BLK), out[:, BLK:].reshape(64, 8, BLK)], axis=1
        )
        second[:, pl.ds(pl.multiple_of(16 * p, 16), 16), :] = both.astype(BF16)
        return carry

    lax.fori_loop(0, PAIRS, second_step, 0)

    encoded = jnp.zeros((128, D), F32)
    for x in range(8):
        copies[x].wait()
        for z in range(0, 8, 2):
            i = 8 * x + z
            lhs = jnp.concatenate([second[i], second[i + 1]], axis=1)
            rhs = jnp.concatenate(
                [patch[:, i].reshape(BLK, D), patch[:, i + 1].reshape(BLK, D)], axis=0
            )
            encoded = encoded + jnp.dot(lhs, rhs, preferred_element_type=F32)

    encoded = encoded.reshape(16, 8, D) + time_ref[...][None]
    space = space_ref[...][None] + along_y_ref[...][:, None, :]
    tokens = (encoded + space).reshape(128, D).astype(BF16)
    tokens_ref[...] = tokens
    wide = tokens.astype(F32)
    scale = lax.rsqrt(jnp.mean(wide * wide, axis=-1, keepdims=True) + 1e-05)
    normed_ref[...] = (wide * scale).astype(BF16)


def attend_kernel(
    place_ref,
    tokens_ref,
    n0_ref,
    n1_ref,
    n2_ref,
    n3_ref,
    wide_ref,
    mixing_ref,
    projector_ref,
    out_ref,
    normed,
    query,
    keys,
    attended,
):
    place = place_ref[0]
    contract = (((1,), (1,)), ((), ()))
    for i, ref in enumerate((n0_ref, n1_ref, n2_ref, n3_ref)):
        normed[128 * i : 128 * (i + 1)] = ref[...]
    query[...] = lax.dot_general(
        normed[0:128], wide_ref[0:D], contract, preferred_element_type=F32
    ).astype(BF16)
    for i in range(4):
        keys[:, 512 * i : 512 * (i + 1)] = lax.dot_general(
            normed[...],
            wide_ref[D + 512 * i : D + 512 * (i + 1)],
            contract,
            preferred_element_type=F32,
        ).astype(BF16)
    col = lax.broadcasted_iota(jnp.int32, (128, 512), 1)
    row = lax.broadcasted_iota(jnp.int32, (128, 512), 0)
    source = place ^ (col // 128)
    allowed = 4 * source + (col % 8) // 2 <= 4 * place + (row % 8) // 2
    for h in range(HEADS):
        q = query[:, HD * h : HD * (h + 1)]
        k = keys[:, HD * h : HD * (h + 1)]
        v = keys[:, D + HD * h : D + HD * (h + 1)]
        scores = lax.dot_general(q, k, contract, preferred_element_type=F32) * (
            1.0 / math.sqrt(HD)
        )
        scores = jnp.where(allowed, scores, -1e30)
        shifted = jnp.exp(scores - jnp.max(scores, axis=-1, keepdims=True))
        weights = shifted * (1.0 / jnp.sum(shifted, axis=-1, keepdims=True))
        attended[:, HD * h : HD * (h + 1)] = jnp.dot(
            weights.astype(BF16), v, preferred_element_type=F32
        ).astype(BF16)
    residual = tokens_ref[...].astype(F32) + lax.dot_general(
        attended[...], mixing_ref[...], contract, preferred_element_type=F32
    )
    scale = lax.rsqrt(jnp.mean(residual * residual, axis=-1, keepdims=True) + 1e-05)
    final = (residual * scale).astype(BF16)
    out_ref[...] = jnp.dot(final, projector_ref[...], preferred_element_type=F32).astype(
        BF16
    )


def vmem():
    return pl.BlockSpec(memory_space=pltpu.VMEM)


def smem():
    return pl.BlockSpec(memory_space=pltpu.SMEM)


def local(
    volume,
    frame_index,
    tile_offset,
    conv_first,
    conv_second,
    patch_weight,
    attend_weight,
    mixing_weight,
    cube_output_projector,
):
    count = lax.axis_size("tile")
    tile_place = lax.axis_index("tile")
    tm_place = lax.axis_index("tm")
    up = [(i, i + 1) for i in range(count - 1)]
    down = [(i + 1, i) for i in range(count - 1)]
    left = lax.ppermute(volume[:, 6:8], "tile", up)
    right = lax.ppermute(volume[:, 0:2], "tile", down)

    wide = lax.all_gather(attend_weight.T, "tile", axis=0, tiled=True)
    mixing = lax.all_gather(mixing_weight.T, "tile", axis=0, tiled=True)

    frequency = jnp.exp(-math.log(1000.0) * jnp.arange(D, dtype=F32) / D)
    phase_shift = (jnp.arange(D) % 2).astype(F32) * (math.pi / 2)
    time_emb = jnp.sin(
        jnp.repeat(frame_index.astype(F32), 2)[:, None] * frequency + phase_shift
    )
    at = lambda axis, place: (tile_offset[axis] + BLOCK_EDGE_UNITS * place).astype(F32)
    along_x = jnp.sin(at(0, tile_place) * frequency)
    along_z = jnp.sin(at(1, jnp.arange(8) % 2)[:, None] * frequency + 1.0)
    along_y = jnp.sin(at(2, jnp.arange(16))[:, None] * frequency + 2.0)

    first = conv_first.transpose(2, 3, 1, 4, 0).reshape(9, 48)
    first = jnp.pad(first, ((0, 7), (0, 0)))
    second = conv_second.transpose(2, 3, 1, 4, 0).reshape(144, 48)
    g, w2 = pl.pallas_call(
        weights_kernel,
        out_shape=(
            jax.ShapeDtypeStruct((9, 48, 256), BF16),
            jax.ShapeDtypeStruct((9, 512, 256), BF16),
        ),
        in_specs=[vmem(), vmem()],
        out_specs=(vmem(), vmem()),
        name="conv_weights",
        compiler_params=pltpu.CompilerParams(vmem_limit_bytes=24 << 20),
    )(first, second)

    tokens, normed = pl.pallas_call(
        encode_kernel,
        out_shape=(
            jax.ShapeDtypeStruct((128, D), BF16),
            jax.ShapeDtypeStruct((128, D), BF16),
        ),
        in_specs=[smem()] + [vmem()] * 8 + [pl.BlockSpec(memory_space=pl.ANY)],
        out_specs=(vmem(), vmem()),
        scratch_shapes=[
            pltpu.VMEM((4, XV, 16, 128), F32),
            pltpu.VMEM((XV, ZV * ROWS, 128), F32),
            pltpu.VMEM((XM, 80, 9 * BLK), BF16),
            pltpu.VMEM((9, 160, 256), BF16),
            pltpu.VMEM((XM, 80, 18 * BLK), BF16),
            pltpu.VMEM((XM, 64, 18 * BLK), BF16),
            pltpu.VMEM((64, 128, BLK), BF16),
            pltpu.VMEM((CH, 64, 8, D), BF16),
            pltpu.SemaphoreType.DMA((8,)),
        ],
        name="encode",
        compiler_params=pltpu.CompilerParams(vmem_limit_bytes=56 << 20),
    )(
        jnp.stack([tile_place, jnp.int32(count)]).astype(jnp.int32),
        volume,
        left,
        right,
        g,
        w2,
        time_emb,
        along_x[None] + along_z,
        along_y,
        patch_weight.reshape(CH, 64, 8, D),
    )

    by_chip = lax.ppermute(normed, "tm", [(0, 2), (2, 0), (1, 3), (3, 1)])
    by_core = lax.ppermute(normed, "tm", [(0, 1), (1, 0), (2, 3), (3, 2)])
    by_both = lax.ppermute(by_chip, "tm", [(0, 1), (1, 0), (2, 3), (3, 2)])

    out = pl.pallas_call(
        attend_kernel,
        out_shape=jax.ShapeDtypeStruct((128, 512), BF16),
        in_specs=[smem()] + [vmem()] * 8,
        out_specs=vmem(),
        scratch_shapes=[
            pltpu.VMEM((512, D), BF16),
            pltpu.VMEM((128, D), BF16),
            pltpu.VMEM((512, 2 * D), BF16),
            pltpu.VMEM((128, D), BF16),
        ],
        name="attend",
        compiler_params=pltpu.CompilerParams(vmem_limit_bytes=48 << 20),
    )(
        tm_place[None].astype(jnp.int32),
        tokens,
        normed,
        by_core,
        by_chip,
        by_both,
        wide,
        mixing,
        cube_output_projector,
    )
    return out.reshape(16, 4, 2, 512).transpose(1, 2, 0, 3)[:, None]


def solution(mesh):
    placed = (
        P("tm", "tile", None, None),
        P("tm"),
        P(),
        P(),
        P(),
        P(),
        P(None, "tile"),
        P(None, "tile"),
        P(),
    )
    return jax.shard_map(
        local,
        mesh=mesh,
        in_specs=placed,
        out_specs=P("tm", "tile", None, None, None),
        check_vma=False,
    )
```

```python
import functools
import math

import jax
import jax.numpy as jnp
from jax import lax
from jax.experimental import pallas as pl
from jax.experimental.pallas import tpu as pltpu
from jax.sharding import PartitionSpec as P

CH = 16
D = 1024
HEADS = 8
HD = 128
BLOCK_EDGE_UNITS = 8

F32 = jnp.float32
BF16 = jnp.bfloat16

ROWS = 8
XV = 12
XM = 10
ZV = 12
ZM = 10
BLK = 128
PAIRS = 8
EARLY = 3


def silu(v):
    return 0.5 * v * (1.0 + jnp.tanh(0.5 * v))


def weights_kernel(first_ref, second_ref, g_ref, w2_ref):
    col = lax.broadcasted_iota(jnp.int32, (48, 768), 1)
    row = lax.broadcasted_iota(jnp.int32, (48, 768), 0)
    spread = (
        ((col // 256) == (row // CH)) & (((col % 128) // 8) == (row % CH))
    ).astype(BF16)
    first = jnp.dot(first_ref[...], spread, preferred_element_type=F32)
    second = jnp.dot(second_ref[...], spread, preferred_element_type=F32).astype(BF16)

    lane = lax.broadcasted_iota(jnp.int32, (48, 256), 1)
    here = lax.broadcasted_iota(jnp.int32, (48, 256), 0) - 16
    out_y = (lane // 128) * 8 + lane % 8
    for tap in range(9):
        total = jnp.zeros((48, 256), F32)
        for k in range(3):
            value = first[tap : tap + 1, 256 * k : 256 * (k + 1)]
            total = total + jnp.where(here == out_y + (k - 1), value, 0.0)
        g_ref[tap] = total.astype(BF16)

    r = lax.broadcasted_iota(jnp.int32, (512, CH), 0)
    c = lax.broadcasted_iota(jnp.int32, (512, CH), 1)
    pick = (((r % 128) // 8) == c).astype(BF16)
    lane = lax.broadcasted_iota(jnp.int32, (512, 256), 1)
    r = lax.broadcasted_iota(jnp.int32, (512, 256), 0)
    shift = (r // 128 - 1) * 8 + r % 8 - ((lane // 128) * 8 + lane % 8)
    for tap in range(9):
        rows = jnp.dot(
            pick, second[CH * tap : CH * (tap + 1)], preferred_element_type=F32
        )
        total = jnp.zeros((512, 256), F32)
        for k in range(3):
            total = total + jnp.where(
                shift == k - 1, rows[:, 256 * k : 256 * (k + 1)], 0.0
            )
        w2_ref[tap] = total.astype(BF16)


def second_convolution(first, last, maps_even, maps_odd, w2_ref, second):
    def second_step(p, carry):
        lanes = pl.ds(pl.multiple_of(256 * p, 256), 512)
        acc = jnp.zeros((512, 256), F32)
        for dx in range(3):
            for dz in range(3):
                if dz == 1:
                    source = maps_odd[dx : dx + 8, :, lanes]
                else:
                    source = maps_even[dx : dx + 8, 8 * dz : 8 * dz + 64, lanes]
                acc = acc + jnp.dot(
                    source.reshape(512, 512), w2_ref[3 * dx + dz], preferred_element_type=F32
                )
        out = silu(acc)
        both = jnp.concatenate(
            [out[:, :BLK].reshape(64, 8, BLK), out[:, BLK:].reshape(64, 8, BLK)], axis=1
        )
        second[:, pl.ds(pl.multiple_of(16 * (p - first), 16), 16), :] = both.astype(BF16)
        return carry

    lax.fori_loop(first, last, second_step, 0)


def convolve_kernel(
    place_ref,
    volume_ref,
    left_ref,
    right_ref,
    g_ref,
    w2_ref,
    second,
    maps_even,
    maps_odd,
    cells,
    planes,
    taps,
    w1,
):
    place = place_ref[0]
    count = place_ref[1]

    cells[:, 0:2] = left_ref[...].astype(F32)
    cells[:, 2:10] = volume_ref[...].astype(F32)
    cells[:, 10:12] = right_ref[...].astype(F32)
    planes[...] = jnp.zeros_like(planes)
    for x in range(XV):
        for f in range(4):
            planes[x, pl.ds(16 + 2 * f, 10, stride=8), :] = cells[f, x, pl.ds(0, 10), :]
            planes[x, pl.ds(2 * f + 1, 10, stride=8), :] = cells[f, x, pl.ds(6, 10), :]
    for dx in range(3):
        for dz in range(3):
            tap = 3 * dx + dz
            for x in range(XM):
                taps[x, :, BLK * tap : BLK * (tap + 1)] = planes[
                    x + dx, 8 * dz : 8 * dz + 80, :
                ].astype(BF16)

    w1[...] = jnp.zeros_like(w1)
    maps_even[:, :, 0:BLK] = jnp.zeros((XM, 80, BLK), BF16)
    maps_even[:, :, 17 * BLK :] = jnp.zeros((XM, 80, BLK), BF16)
    maps_odd[:, :, 0:BLK] = jnp.zeros((XM, 64, BLK), BF16)
    maps_odd[:, :, 17 * BLK :] = jnp.zeros((XM, 64, BLK), BF16)

    x = lax.broadcasted_iota(jnp.int32, (XM, 80, 1), 0) + 8 * place - 1
    r = lax.broadcasted_iota(jnp.int32, (XM, 80, 1), 1)
    z = 8 * (r % 2) + r // 8 - 1
    inside = (x >= 0) & (x < 8 * count) & (z >= 0) & (z < 16)

    def first_step(n, carry):
        before = pl.ds(pl.multiple_of(16 * jnp.maximum(n - 1, 0), 16), 16)
        now = pl.ds(pl.multiple_of(16 * n, 16), 48)
        for tap in range(9):
            w1[tap, before, :] = jnp.zeros((16, 256), BF16)
            w1[tap, now, :] = g_ref[tap]
        acc = jnp.zeros((XM * 80, 256), F32)
        for tap in range(9):
            acc = acc + jnp.dot(
                taps[:, :, BLK * tap : BLK * (tap + 1)].reshape(XM * 80, BLK),
                w1[tap, 16:144, :],
                preferred_element_type=F32,
            )
        out = jnp.where(inside, silu(acc).reshape(XM, 80, 256), 0.0)
        lanes = pl.ds(pl.multiple_of(256 * n + BLK, BLK), 256)
        maps_even[:, :, lanes] = out.astype(BF16)
        maps_odd[:, :, lanes] = out[:, 8:72].astype(BF16)
        return carry

    lax.fori_loop(0, PAIRS, first_step, 0)

    second_convolution(0, EARLY, maps_even, maps_odd, w2_ref, second)


def patch_kernel(
    early,
    maps_even,
    maps_odd,
    w2_ref,
    time_ref,
    space_ref,
    along_y_ref,
    patch_hbm,
    tokens_ref,
    normed_ref,
    late,
    patch,
    patch_sem,
):
    copies = [
        pltpu.make_async_copy(
            patch_hbm.at[:, pl.ds(8 * i, 8)],
            patch.at[:, pl.ds(8 * i, 8)],
            patch_sem.at[i],
        )
        for i in range(8)
    ]
    for copy in copies:
        copy.start()
    second_convolution(EARLY, PAIRS, maps_even, maps_odd, w2_ref, late)
    encoded = jnp.zeros((128, D), F32)
    for x in range(8):
        copies[x].wait()
        for z in range(0, 8, 2):
            i = 8 * x + z
            lhs = jnp.concatenate(
                [jnp.concatenate([early[j], late[j]], axis=0) for j in (i, i + 1)], axis=1
            )
            rhs = jnp.concatenate(
                [patch[:, i].reshape(BLK, D), patch[:, i + 1].reshape(BLK, D)], axis=0
            )
            encoded = encoded + jnp.dot(lhs, rhs, preferred_element_type=F32)

    encoded = encoded.reshape(16, 8, D) + time_ref[...][None]
    space = space_ref[...][None] + along_y_ref[...][:, None, :]
    tokens = (encoded + space).reshape(128, D).astype(BF16)
    tokens_ref[...] = tokens
    wide = tokens.astype(F32)
    scale = lax.rsqrt(jnp.mean(wide * wide, axis=-1, keepdims=True) + 1e-05)
    normed_ref[...] = (wide * scale).astype(BF16)


def pair_kernel(at_ref, own_ref, other_ref, by_z_ref, by_x_ref):
    high = at_ref[1]
    for a, ref in enumerate((by_z_ref, by_x_ref)):
        ref[pl.ds(high, 1)] = own_ref[a : a + 1]
        ref[pl.ds(1 - high, 1)] = other_ref[a : a + 1]


def plane_kernel(at_ref, z0, z1, z3, z2, x0, x1, x3, x2, by_z_ref, by_x_ref):
    for i, ref in enumerate((z0, z1, z2, z3)):
        by_z_ref[:, pl.ds((at_ref[2] + 4 - i) % 4, 1)] = ref[...][:, None]
    for i, ref in enumerate((x0, x1, x2, x3)):
        by_x_ref[pl.ds((at_ref[0] + 4 - i) % 4, 1)] = ref[...][None]


def attend_kernel(
    place_ref,
    at_ref,
    tokens_ref,
    n0_ref,
    n1_ref,
    n2_ref,
    n3_ref,
    projector_ref,
    *rest,
):
    parts = rest[:16]
    out_ref, wide, mixing, sems, normed, query, keys, attended = rest[16:]
    copies = []
    for i, part in enumerate(parts):
        core = at_ref[3] if i < 8 else 1 - at_ref[3]
        quarter = 2 * core + (i % 8) // 4
        if i % 8 < 4:
            spot = (at_ref[0] + 4 - i % 4) % 4
            ends = [w.at[spot, :, :, quarter] for w in (wide, mixing)]
        else:
            spot = (at_ref[2] + 4 - i % 4) % 4
            ends = [w.at[:, :, spot, quarter] for w in (wide, mixing)]
        starts = [part.at[:, :, 0:3], part.at[:, :, 3:4]]
        for j in range(2):
            copies.append(pltpu.make_async_copy(starts[j], ends[j], sems.at[2 * i + j]))
    for copy in copies:
        copy.start()
    place = place_ref[0]
    contract = (((1,), (1,)), ((), ()))
    for i, ref in enumerate((n0_ref, n1_ref, n2_ref, n3_ref)):
        normed[128 * i : 128 * (i + 1)] = ref[...]
    for copy in copies:
        copy.wait()
    columns = wide.reshape(384, 8, D)
    query[...] = lax.dot_general(
        normed[0:128], columns[0:128].reshape(D, D), contract, preferred_element_type=F32
    ).astype(BF16)
    for i in range(4):
        keys[:, 512 * i : 512 * (i + 1)] = lax.dot_general(
            normed[...],
            columns[128 + 64 * i : 128 + 64 * (i + 1)].reshape(512, D),
            contract,
            preferred_element_type=F32,
        ).astype(BF16)
    col = lax.broadcasted_iota(jnp.int32, (128, 512), 1)
    row = lax.broadcasted_iota(jnp.int32, (128, 512), 0)
    source = place ^ (col // 128)
    allowed = 4 * source + (col % 8) // 2 <= 4 * place + (row % 8) // 2
    for h in range(HEADS):
        q = query[:, HD * h : HD * (h + 1)]
        k = keys[:, HD * h : HD * (h + 1)]
        v = keys[:, D + HD * h : D + HD * (h + 1)]
        scores = lax.dot_general(q, k, contract, preferred_element_type=F32) * (
            1.0 / math.sqrt(HD)
        )
        scores = jnp.where(allowed, scores, -1e30)
        shifted = jnp.exp(scores - jnp.max(scores, axis=-1, keepdims=True))
        weights = shifted * (1.0 / jnp.sum(shifted, axis=-1, keepdims=True))
        attended[:, HD * h : HD * (h + 1)] = jnp.dot(
            weights.astype(BF16), v, preferred_element_type=F32
        ).astype(BF16)
    residual = tokens_ref[...].astype(F32) + lax.dot_general(
        attended[...], mixing[...].reshape(D, D), contract, preferred_element_type=F32
    )
    scale = lax.rsqrt(jnp.mean(residual * residual, axis=-1, keepdims=True) + 1e-05)
    final = (residual * scale).astype(BF16)
    out_ref[...] = jnp.dot(final, projector_ref[...], preferred_element_type=F32).astype(
        BF16
    )


def vmem():
    return pl.BlockSpec(memory_space=pltpu.VMEM)


def smem():
    return pl.BlockSpec(memory_space=pltpu.SMEM)


def send(array, where):
    pairs = []
    for x in range(4):
        for y in range(4):
            for z in range(4):
                for c in range(2):
                    ends = []
                    for a, b, d, e in ((x, y, z, c), where(x, y, z, c)):
                        a, b, d = a % 4, b % 4, d % 4
                        ends.append(4 * (8 * a + 4 * (b // 2) + d) + 2 * (b % 2) + e)
                    pairs.append(tuple(ends))
    return lax.ppermute(array, ("tile", "tm"), pairs)


def local(
    volume,
    frame_index,
    tile_offset,
    conv_first,
    conv_second,
    patch_weight,
    attend_weight,
    mixing_weight,
    cube_output_projector,
):
    count = lax.axis_size("tile")
    tile_place = lax.axis_index("tile")
    tm_place = lax.axis_index("tm")
    up = [(i, i + 1) for i in range(count - 1)]
    down = [(i + 1, i) for i in range(count - 1)]
    left = lax.ppermute(volume[:, 6:8], "tile", up)
    right = lax.ppermute(volume[:, 0:2], "tile", down)

    core = tm_place % 2
    at = jnp.stack([tile_place // 8, (tile_place // 4) % 2, tile_place % 4, core])
    at = at.astype(jnp.int32)
    shard = jnp.concatenate(
        [attend_weight.T.reshape(4, 3, 8, D), mixing_weight.T.reshape(4, 1, 8, D)], axis=1
    )
    shard = lax.dynamic_slice_in_dim(shard, 2 * core, 2, axis=0)
    other = send(shard, lambda x, y, z, c: (x, 3 - y, z, c))
    unit = jax.ShapeDtypeStruct((2, 4, 8, D), BF16)
    by_z, by_x = pl.pallas_call(
        pair_kernel,
        out_shape=(unit, unit),
        in_specs=[smem(), vmem(), vmem()],
        out_specs=(vmem(), vmem()),
        name="pairs",
    )(at, shard, other)
    planes = [by_z] + [
        send(by_z, lambda x, y, z, c, k=k: (x, y, z + k, c)) for k in (1, 3, 2)
    ]
    planes += [by_x] + [
        send(by_x, lambda x, y, z, c, k=k: (x + k, y, z, c)) for k in (1, 3, 2)
    ]
    by_z, by_x = pl.pallas_call(
        plane_kernel,
        out_shape=(
            jax.ShapeDtypeStruct((2, 4, 4, 8, D), BF16),
            jax.ShapeDtypeStruct((4, 2, 4, 8, D), BF16),
        ),
        in_specs=[smem()] + [vmem()] * 8,
        out_specs=(vmem(), vmem()),
        name="planes",
        compiler_params=pltpu.CompilerParams(vmem_limit_bytes=8 << 20),
    )(at, *planes)
    volume, left, right, by_z, by_x = lax.optimization_barrier(
        (volume, left, right, by_z, by_x)
    )
    x_step = lambda part, k: send(part, lambda x, y, z, c: (x + k, y, z, c))
    z_step = lambda part, k: send(part, lambda x, y, z, c: (x, y, z + k, c))
    along = {k: x_step(by_z, k) for k in (1, 3)}
    across = {k: z_step(by_x, k) for k in (1, 3)}

    frequency = jnp.exp(-math.log(1000.0) * jnp.arange(D, dtype=F32) / D)
    phase_shift = (jnp.arange(D) % 2).astype(F32) * (math.pi / 2)
    time_emb = jnp.sin(
        jnp.repeat(frame_index.astype(F32), 2)[:, None] * frequency + phase_shift
    )
    spot = lambda axis, place: (tile_offset[axis] + BLOCK_EDGE_UNITS * place).astype(F32)
    along_x = jnp.sin(spot(0, tile_place) * frequency)
    along_z = jnp.sin(spot(1, jnp.arange(8) % 2)[:, None] * frequency + 1.0)
    along_y = jnp.sin(spot(2, jnp.arange(16))[:, None] * frequency + 2.0)

    first = conv_first.transpose(2, 3, 1, 4, 0).reshape(9, 48)
    first = jnp.pad(first, ((0, 7), (0, 0)))
    second = conv_second.transpose(2, 3, 1, 4, 0).reshape(144, 48)
    g, w2 = pl.pallas_call(
        weights_kernel,
        out_shape=(
            jax.ShapeDtypeStruct((9, 48, 256), BF16),
            jax.ShapeDtypeStruct((9, 512, 256), BF16),
        ),
        in_specs=[vmem(), vmem()],
        out_specs=(vmem(), vmem()),
        name="conv_weights",
        compiler_params=pltpu.CompilerParams(vmem_limit_bytes=12 << 20),
    )(first, second)

    early, even, odd = pl.pallas_call(
        convolve_kernel,
        out_shape=(
            jax.ShapeDtypeStruct((64, 16 * EARLY, BLK), BF16),
            jax.ShapeDtypeStruct((XM, 80, 18 * BLK), BF16),
            jax.ShapeDtypeStruct((XM, 64, 18 * BLK), BF16),
        ),
        in_specs=[smem()] + [vmem()] * 5,
        out_specs=(vmem(),) * 3,
        scratch_shapes=[
            pltpu.VMEM((4, XV, 16, 128), F32),
            pltpu.VMEM((XV, ZV * ROWS, 128), F32),
            pltpu.VMEM((XM, 80, 9 * BLK), BF16),
            pltpu.VMEM((9, 160, 256), BF16),
        ],
        name="convolve",
        compiler_params=pltpu.CompilerParams(vmem_limit_bytes=16 << 20),
        cost_estimate=pl.CostEstimate(
            flops=15_000_000_000, transcendentals=3_000_000, bytes_accessed=8_000_000
        ),
    )(
        jnp.stack([tile_place, jnp.int32(count)]).astype(jnp.int32),
        volume,
        left,
        right,
        g,
        w2,
    )
    early, by_z, by_x, along[1], along[3], across[1], across[3] = (
        lax.optimization_barrier(
            (early, by_z, by_x, along[1], along[3], across[1], across[3])
        )
    )
    along[2] = x_step(by_z, 2)
    across[2] = z_step(by_x, 2)
    tokens, normed = pl.pallas_call(
        patch_kernel,
        out_shape=(
            jax.ShapeDtypeStruct((128, D), BF16),
            jax.ShapeDtypeStruct((128, D), BF16),
        ),
        in_specs=[vmem()] * 7 + [pl.BlockSpec(memory_space=pl.ANY)],
        out_specs=(vmem(), vmem()),
        scratch_shapes=[
            pltpu.VMEM((64, 16 * (PAIRS - EARLY), BLK), BF16),
            pltpu.VMEM((CH, 64, 8, D), BF16),
            pltpu.SemaphoreType.DMA((8,)),
        ],
        name="patches",
        compiler_params=pltpu.CompilerParams(vmem_limit_bytes=28 << 20),
        cost_estimate=pl.CostEstimate(
            flops=0, transcendentals=0, bytes_accessed=1_000
        ),
    )(
        early,
        even,
        odd,
        w2,
        time_emb,
        along_x[None] + along_z,
        along_y,
        patch_weight.reshape(CH, 64, 8, D),
    )

    parts = [by_z, along[1], along[2], along[3], by_x, across[1], across[2], across[3]]
    normed, *parts = lax.optimization_barrier((normed, *parts))
    parts += [send(part, lambda x, y, z, c: (x, y, z, 1 - c)) for part in parts]
    by_chip = lax.ppermute(normed, "tm", [(0, 2), (2, 0), (1, 3), (3, 1)])
    by_core = lax.ppermute(normed, "tm", [(0, 1), (1, 0), (2, 3), (3, 2)])
    by_both = lax.ppermute(by_chip, "tm", [(0, 1), (1, 0), (2, 3), (3, 2)])

    out = pl.pallas_call(
        attend_kernel,
        out_shape=jax.ShapeDtypeStruct((128, 512), BF16),
        in_specs=[smem()] * 2
        + [vmem()] * 6
        + [pl.BlockSpec(memory_space=pl.ANY)] * len(parts),
        out_specs=vmem(),
        scratch_shapes=[
            pltpu.VMEM((4, 2, 4, 4, 3, 8, D), BF16),
            pltpu.VMEM((4, 2, 4, 4, 1, 8, D), BF16),
            pltpu.SemaphoreType.DMA((2 * len(parts),)),
            pltpu.VMEM((512, D), BF16),
            pltpu.VMEM((128, D), BF16),
            pltpu.VMEM((512, 2 * D), BF16),
            pltpu.VMEM((128, D), BF16),
        ],
        name="attend",
        compiler_params=pltpu.CompilerParams(vmem_limit_bytes=26 << 20),
    )(
        tm_place[None].astype(jnp.int32),
        at,
        tokens,
        normed,
        by_core,
        by_chip,
        by_both,
        cube_output_projector,
        *parts,
    )
    return out.reshape(16, 4, 2, 512).transpose(1, 2, 0, 3)[:, None]


def solution(mesh):
    placed = (
        P("tm", "tile", None, None),
        P("tm"),
        P(),
        P(),
        P(),
        P(),
        P(None, "tile"),
        P(None, "tile"),
        P(),
    )
    return jax.shard_map(
        local,
        mesh=mesh,
        in_specs=placed,
        out_specs=P("tm", "tile", None, None, None),
        check_vma=False,
    )
```

```python
import functools
import math

import jax
import jax.numpy as jnp
from jax import lax
from jax.experimental import pallas as pl
from jax.experimental.pallas import tpu as pltpu
from jax.sharding import PartitionSpec as P

CH = 16
D = 1024
HEADS = 8
HD = 128
BLOCK_EDGE_UNITS = 8

F32 = jnp.float32
BF16 = jnp.bfloat16

ROWS = 8
XV = 12
XM = 10
ZV = 12
ZM = 10
BLK = 128
PAIRS = 8


def silu(v):
    return 0.5 * v * (1.0 + jnp.tanh(0.5 * v))


def weights_kernel(first_ref, second_ref, g_ref, w2_ref):
    col = lax.broadcasted_iota(jnp.int32, (48, 768), 1)
    row = lax.broadcasted_iota(jnp.int32, (48, 768), 0)
    spread = (
        ((col // 256) == (row // CH)) & (((col % 128) // 8) == (row % CH))
    ).astype(BF16)
    first = jnp.dot(first_ref[...], spread, preferred_element_type=F32)
    second = jnp.dot(second_ref[...], spread, preferred_element_type=F32).astype(BF16)

    lane = lax.broadcasted_iota(jnp.int32, (48, 256), 1)
    here = lax.broadcasted_iota(jnp.int32, (48, 256), 0) - 16
    out_y = (lane // 128) * 8 + lane % 8
    for tap in range(9):
        total = jnp.zeros((48, 256), F32)
        for k in range(3):
            value = first[tap : tap + 1, 256 * k : 256 * (k + 1)]
            total = total + jnp.where(here == out_y + (k - 1), value, 0.0)
        g_ref[tap] = total.astype(BF16)

    r = lax.broadcasted_iota(jnp.int32, (512, CH), 0)
    c = lax.broadcasted_iota(jnp.int32, (512, CH), 1)
    pick = (((r % 128) // 8) == c).astype(BF16)
    lane = lax.broadcasted_iota(jnp.int32, (512, 256), 1)
    r = lax.broadcasted_iota(jnp.int32, (512, 256), 0)
    shift = (r // 128 - 1) * 8 + r % 8 - ((lane // 128) * 8 + lane % 8)
    for tap in range(9):
        rows = jnp.dot(
            pick, second[CH * tap : CH * (tap + 1)], preferred_element_type=F32
        )
        total = jnp.zeros((512, 256), F32)
        for k in range(3):
            total = total + jnp.where(
                shift == k - 1, rows[:, 256 * k : 256 * (k + 1)], 0.0
            )
        w2_ref[tap] = total.astype(BF16)


def second_convolution(maps_even, maps_odd, w2_ref, second):
    def second_step(p, carry):
        lanes = pl.ds(pl.multiple_of(256 * p, 256), 512)
        acc = jnp.zeros((512, 256), F32)
        for dx in range(3):
            for dz in range(3):
                if dz == 1:
                    source = maps_odd[dx : dx + 8, :, lanes]
                else:
                    source = maps_even[dx : dx + 8, 8 * dz : 8 * dz + 64, lanes]
                acc = acc + jnp.dot(
                    source.reshape(512, 512), w2_ref[3 * dx + dz], preferred_element_type=F32
                )
        out = silu(acc)
        both = jnp.concatenate(
            [out[:, :BLK].reshape(64, 8, BLK), out[:, BLK:].reshape(64, 8, BLK)], axis=1
        )
        second[:, pl.ds(pl.multiple_of(16 * p, 16), 16), :] = both.astype(BF16)
        return carry

    lax.fori_loop(0, PAIRS, second_step, 0)


def encode_kernel(
    place_ref,
    volume_ref,
    left_ref,
    right_ref,
    g_ref,
    w2_ref,
    time_ref,
    space_ref,
    along_y_ref,
    patch_hbm,
    tokens_ref,
    normed_ref,
    second,
    maps_even,
    maps_odd,
    cells,
    planes,
    taps,
    w1,
    patch,
    patch_sem,
):
    copies = [
        pltpu.make_async_copy(
            patch_hbm.at[:, pl.ds(8 * i, 8)],
            patch.at[:, pl.ds(8 * i, 8)],
            patch_sem.at[i],
        )
        for i in range(8)
    ]
    for copy in copies:
        copy.start()
    place = place_ref[0]
    count = place_ref[1]

    cells[:, 0:2] = left_ref[...].astype(F32)
    cells[:, 2:10] = volume_ref[...].astype(F32)
    cells[:, 10:12] = right_ref[...].astype(F32)
    planes[...] = jnp.zeros_like(planes)
    for x in range(XV):
        for f in range(4):
            planes[x, pl.ds(16 + 2 * f, 10, stride=8), :] = cells[f, x, pl.ds(0, 10), :]
            planes[x, pl.ds(2 * f + 1, 10, stride=8), :] = cells[f, x, pl.ds(6, 10), :]
    for dx in range(3):
        for dz in range(3):
            tap = 3 * dx + dz
            for x in range(XM):
                taps[x, :, BLK * tap : BLK * (tap + 1)] = planes[
                    x + dx, 8 * dz : 8 * dz + 80, :
                ].astype(BF16)

    w1[...] = jnp.zeros_like(w1)
    maps_even[:, :, 0:BLK] = jnp.zeros((XM, 80, BLK), BF16)
    maps_even[:, :, 17 * BLK :] = jnp.zeros((XM, 80, BLK), BF16)
    maps_odd[:, :, 0:BLK] = jnp.zeros((XM, 64, BLK), BF16)
    maps_odd[:, :, 17 * BLK :] = jnp.zeros((XM, 64, BLK), BF16)

    x = lax.broadcasted_iota(jnp.int32, (XM, 80, 1), 0) + 8 * place - 1
    r = lax.broadcasted_iota(jnp.int32, (XM, 80, 1), 1)
    z = 8 * (r % 2) + r // 8 - 1
    inside = (x >= 0) & (x < 8 * count) & (z >= 0) & (z < 16)

    def first_step(n, carry):
        before = pl.ds(pl.multiple_of(16 * jnp.maximum(n - 1, 0), 16), 16)
        now = pl.ds(pl.multiple_of(16 * n, 16), 48)
        for tap in range(9):
            w1[tap, before, :] = jnp.zeros((16, 256), BF16)
            w1[tap, now, :] = g_ref[tap]
        acc = jnp.zeros((XM * 80, 256), F32)
        for tap in range(9):
            acc = acc + jnp.dot(
                taps[:, :, BLK * tap : BLK * (tap + 1)].reshape(XM * 80, BLK),
                w1[tap, 16:144, :],
                preferred_element_type=F32,
            )
        out = jnp.where(inside, silu(acc).reshape(XM, 80, 256), 0.0)
        lanes = pl.ds(pl.multiple_of(256 * n + BLK, BLK), 256)
        maps_even[:, :, lanes] = out.astype(BF16)
        maps_odd[:, :, lanes] = out[:, 8:72].astype(BF16)
        return carry

    lax.fori_loop(0, PAIRS, first_step, 0)

    second_convolution(maps_even, maps_odd, w2_ref, second)
    encoded = jnp.zeros((128, D), F32)
    for x in range(8):
        copies[x].wait()
        for z in range(0, 8, 2):
            i = 8 * x + z
            lhs = jnp.concatenate([second[i], second[i + 1]], axis=1)
            rhs = jnp.concatenate(
                [patch[:, i].reshape(BLK, D), patch[:, i + 1].reshape(BLK, D)], axis=0
            )
            encoded = encoded + jnp.dot(lhs, rhs, preferred_element_type=F32)

    encoded = encoded.reshape(16, 8, D) + time_ref[...][None]
    space = space_ref[...][None] + along_y_ref[...][:, None, :]
    tokens = (encoded + space).reshape(128, D).astype(BF16)
    tokens_ref[...] = tokens
    wide = tokens.astype(F32)
    scale = lax.rsqrt(jnp.mean(wide * wide, axis=-1, keepdims=True) + 1e-05)
    normed_ref[...] = (wide * scale).astype(BF16)


def pair_kernel(at_ref, own_ref, other_ref, pair_ref):
    high = at_ref[1]
    pair_ref[pl.ds(high, 1)] = own_ref[...][None]
    pair_ref[pl.ds(1 - high, 1)] = other_ref[...][None]


def plane_kernel(at_ref, own_ref, one_ref, three_ref, two_ref, plane_ref):
    spot = jnp.where(at_ref[3] == 0, at_ref[2], at_ref[0])
    for i, ref in enumerate((own_ref, one_ref, two_ref, three_ref)):
        plane_ref[pl.ds((spot + 4 - i) % 4, 1)] = ref[...][None]


def attend_kernel(
    place_ref,
    at_ref,
    tokens_ref,
    n0_ref,
    n1_ref,
    n2_ref,
    n3_ref,
    projector_ref,
    *rest,
):
    parts = rest[:8]
    out_ref, wide, mixing, sems, normed, query, keys, attended = rest[8:]

    def copies(core):
        out = []
        for i, part in enumerate(parts):
            owner = core if i < 4 else 1 - core
            spot = (at_ref[2 * owner] + 4 - i % 4) % 4
            for high in range(2):
                for j, weight in enumerate((wide, mixing)):
                    if owner == 0:
                        end = weight.at[spot, high, :, owner]
                    else:
                        end = weight.at[:, high, spot, owner]
                    start = part.at[:, high, 0:6] if j == 0 else part.at[:, high, 6:8]
                    out.append(
                        pltpu.make_async_copy(start, end, sems.at[4 * i + 2 * high + j])
                    )
        return out

    for core in range(2):

        @pl.when(at_ref[3] == core)
        def _():
            for copy in copies(core):
                copy.start()

    place = place_ref[0]
    contract = (((1,), (1,)), ((), ()))
    for i, ref in enumerate((n0_ref, n1_ref, n2_ref, n3_ref)):
        normed[128 * i : 128 * (i + 1)] = ref[...]
    for core in range(2):

        @pl.when(at_ref[3] == core)
        def _():
            for copy in copies(core):
                copy.wait()

    columns = wide.reshape(384, 8, D)
    query[...] = lax.dot_general(
        normed[0:128], columns[0:128].reshape(D, D), contract, preferred_element_type=F32
    ).astype(BF16)
    for i in range(4):
        keys[:, 512 * i : 512 * (i + 1)] = lax.dot_general(
            normed[...],
            columns[128 + 64 * i : 128 + 64 * (i + 1)].reshape(512, D),
            contract,
            preferred_element_type=F32,
        ).astype(BF16)
    col = lax.broadcasted_iota(jnp.int32, (128, 512), 1)
    row = lax.broadcasted_iota(jnp.int32, (128, 512), 0)
    source = place ^ (col // 128)
    allowed = 4 * source + (col % 8) // 2 <= 4 * place + (row % 8) // 2
    for h in range(HEADS):
        q = query[:, HD * h : HD * (h + 1)]
        k = keys[:, HD * h : HD * (h + 1)]
        v = keys[:, D + HD * h : D + HD * (h + 1)]
        scores = lax.dot_general(q, k, contract, preferred_element_type=F32) * (
            1.0 / math.sqrt(HD)
        )
        scores = jnp.where(allowed, scores, -1e30)
        shifted = jnp.exp(scores - jnp.max(scores, axis=-1, keepdims=True))
        weights = shifted * (1.0 / jnp.sum(shifted, axis=-1, keepdims=True))
        attended[:, HD * h : HD * (h + 1)] = jnp.dot(
            weights.astype(BF16), v, preferred_element_type=F32
        ).astype(BF16)
    residual = tokens_ref[...].astype(F32) + lax.dot_general(
        attended[...], mixing[...].reshape(D, D), contract, preferred_element_type=F32
    )
    scale = lax.rsqrt(jnp.mean(residual * residual, axis=-1, keepdims=True) + 1e-05)
    final = (residual * scale).astype(BF16)
    out_ref[...] = jnp.dot(final, projector_ref[...], preferred_element_type=F32).astype(
        BF16
    )


def vmem():
    return pl.BlockSpec(memory_space=pltpu.VMEM)


def smem():
    return pl.BlockSpec(memory_space=pltpu.SMEM)


def send(array, where):
    pairs = []
    for x in range(4):
        for y in range(4):
            for z in range(4):
                for c in range(2):
                    ends = []
                    for a, b, d, e in ((x, y, z, c), where(x, y, z, c)):
                        a, b, d = a % 4, b % 4, d % 4
                        ends.append(4 * (8 * a + 4 * (b // 2) + d) + 2 * (b % 2) + e)
                    pairs.append(tuple(ends))
    return lax.ppermute(array, ("tile", "tm"), pairs)


def local(
    volume,
    frame_index,
    tile_offset,
    conv_first,
    conv_second,
    patch_weight,
    attend_weight,
    mixing_weight,
    cube_output_projector,
):
    count = lax.axis_size("tile")
    tile_place = lax.axis_index("tile")
    tm_place = lax.axis_index("tm")
    up = [(i, i + 1) for i in range(count - 1)]
    down = [(i + 1, i) for i in range(count - 1)]
    left = lax.ppermute(volume[:, 6:8], "tile", up)
    right = lax.ppermute(volume[:, 0:2], "tile", down)

    core = tm_place % 2
    at = jnp.stack([tile_place // 8, (tile_place // 4) % 2, tile_place % 4, core])
    at = at.astype(jnp.int32)
    shard = jnp.concatenate(
        [attend_weight.T.reshape(2, 6, 8, D), mixing_weight.T.reshape(2, 2, 8, D)], axis=1
    )
    shard = lax.dynamic_index_in_dim(shard, core, axis=0, keepdims=False)
    other = send(shard, lambda x, y, z, c: (x, 3 - y, z, c))
    pair = pl.pallas_call(
        pair_kernel,
        out_shape=jax.ShapeDtypeStruct((2, 8, 8, D), BF16),
        in_specs=[smem(), vmem(), vmem()],
        out_specs=vmem(),
        name="pairs",
    )(at, shard, other)
    line = lambda part, k: send(
        part, lambda x, y, z, c: (x + k * c, y, z + k * (1 - c), c)
    )
    cross = lambda part, k: send(
        part, lambda x, y, z, c: (x + k * (1 - c), y, z + k * c, c)
    )
    swap = lambda part: send(part, lambda x, y, z, c: (x, y, z, 1 - c))
    plane = pl.pallas_call(
        plane_kernel,
        out_shape=jax.ShapeDtypeStruct((4, 2, 8, 8, D), BF16),
        in_specs=[smem()] + [vmem()] * 4,
        out_specs=vmem(),
        name="planes",
        compiler_params=pltpu.CompilerParams(vmem_limit_bytes=8 << 20),
    )(at, pair, line(pair, 1), line(pair, 3), line(pair, 2))
    volume, left, right, plane = lax.optimization_barrier((volume, left, right, plane))
    one, two, three = cross(plane, 1), cross(plane, 2), cross(plane, 3)
    swapped = swap(plane)

    frequency = jnp.exp(-math.log(1000.0) * jnp.arange(D, dtype=F32) / D)
    phase_shift = (jnp.arange(D) % 2).astype(F32) * (math.pi / 2)
    time_emb = jnp.sin(
        jnp.repeat(frame_index.astype(F32), 2)[:, None] * frequency + phase_shift
    )
    spot = lambda axis, place: (tile_offset[axis] + BLOCK_EDGE_UNITS * place).astype(F32)
    along_x = jnp.sin(spot(0, tile_place) * frequency)
    along_z = jnp.sin(spot(1, jnp.arange(8) % 2)[:, None] * frequency + 1.0)
    along_y = jnp.sin(spot(2, jnp.arange(16))[:, None] * frequency + 2.0)

    first = conv_first.transpose(2, 3, 1, 4, 0).reshape(9, 48)
    first = jnp.pad(first, ((0, 7), (0, 0)))
    second = conv_second.transpose(2, 3, 1, 4, 0).reshape(144, 48)
    g, w2 = pl.pallas_call(
        weights_kernel,
        out_shape=(
            jax.ShapeDtypeStruct((9, 48, 256), BF16),
            jax.ShapeDtypeStruct((9, 512, 256), BF16),
        ),
        in_specs=[vmem(), vmem()],
        out_specs=(vmem(), vmem()),
        name="conv_weights",
        compiler_params=pltpu.CompilerParams(vmem_limit_bytes=12 << 20),
    )(first, second)

    tokens, normed = pl.pallas_call(
        encode_kernel,
        out_shape=(
            jax.ShapeDtypeStruct((128, D), BF16),
            jax.ShapeDtypeStruct((128, D), BF16),
        ),
        in_specs=[smem()] + [vmem()] * 8 + [pl.BlockSpec(memory_space=pl.ANY)],
        out_specs=(vmem(), vmem()),
        scratch_shapes=[
            pltpu.VMEM((64, 128, BLK), BF16),
            pltpu.VMEM((XM, 80, 18 * BLK), BF16),
            pltpu.VMEM((XM, 64, 18 * BLK), BF16),
            pltpu.VMEM((4, XV, 16, 128), F32),
            pltpu.VMEM((XV, ZV * ROWS, 128), F32),
            pltpu.VMEM((XM, 80, 9 * BLK), BF16),
            pltpu.VMEM((9, 160, 256), BF16),
            pltpu.VMEM((CH, 64, 8, D), BF16),
            pltpu.SemaphoreType.DMA((8,)),
        ],
        name="encode",
        compiler_params=pltpu.CompilerParams(vmem_limit_bytes=40 << 20),
        cost_estimate=pl.CostEstimate(
            flops=15_000_000_000, transcendentals=3_000_000, bytes_accessed=20_000_000
        ),
    )(
        jnp.stack([tile_place, jnp.int32(count)]).astype(jnp.int32),
        volume,
        left,
        right,
        g,
        w2,
        time_emb,
        along_x[None] + along_z,
        along_y,
        patch_weight.reshape(CH, 64, 8, D),
    )
    normed, one, two, three, swapped = lax.optimization_barrier(
        (normed, one, two, three, swapped)
    )
    parts = [plane, one, two, three, swapped, swap(one), swap(two), swap(three)]
    by_chip = lax.ppermute(normed, "tm", [(0, 2), (2, 0), (1, 3), (3, 1)])
    by_core = lax.ppermute(normed, "tm", [(0, 1), (1, 0), (2, 3), (3, 2)])
    by_both = lax.ppermute(by_chip, "tm", [(0, 1), (1, 0), (2, 3), (3, 2)])

    out = pl.pallas_call(
        attend_kernel,
        out_shape=jax.ShapeDtypeStruct((128, 512), BF16),
        in_specs=[smem()] * 2
        + [vmem()] * 6
        + [pl.BlockSpec(memory_space=pl.ANY)] * len(parts),
        out_specs=vmem(),
        scratch_shapes=[
            pltpu.VMEM((4, 2, 4, 2, 6, 8, D), BF16),
            pltpu.VMEM((4, 2, 4, 2, 2, 8, D), BF16),
            pltpu.SemaphoreType.DMA((4 * len(parts),)),
            pltpu.VMEM((512, D), BF16),
            pltpu.VMEM((128, D), BF16),
            pltpu.VMEM((512, 2 * D), BF16),
            pltpu.VMEM((128, D), BF16),
        ],
        name="attend",
        compiler_params=pltpu.CompilerParams(vmem_limit_bytes=26 << 20),
    )(
        tm_place[None].astype(jnp.int32),
        at,
        tokens,
        normed,
        by_core,
        by_chip,
        by_both,
        cube_output_projector,
        *parts,
    )
    return out.reshape(16, 4, 2, 512).transpose(1, 2, 0, 3)[:, None]


def solution(mesh):
    placed = (
        P("tm", "tile", None, None),
        P("tm"),
        P(),
        P(),
        P(),
        P(),
        P(None, "tile"),
        P(None, "tile"),
        P(),
    )
    return jax.shard_map(
        local,
        mesh=mesh,
        in_specs=placed,
        out_specs=P("tm", "tile", None, None, None),
        check_vma=False,
    )
```

```python
import functools
import math

import jax
import jax.numpy as jnp
from jax import lax
from jax.experimental import pallas as pl
from jax.experimental.pallas import tpu as pltpu
from jax.sharding import PartitionSpec as P

CH = 16
D = 1024
HEADS = 8
HD = 128
BLOCK_EDGE_UNITS = 8

F32 = jnp.float32
BF16 = jnp.bfloat16

ROWS = 8
XV = 12
XM = 10
ZV = 12
ZM = 10
BLK = 128
PAIRS = 8


def silu(v):
    return 0.5 * v * (1.0 + jnp.tanh(0.5 * v))


def weights_kernel(first_ref, second_ref, g_ref, w2_ref):
    col = lax.broadcasted_iota(jnp.int32, (48, 768), 1)
    row = lax.broadcasted_iota(jnp.int32, (48, 768), 0)
    spread = (
        ((col // 256) == (row // CH)) & (((col % 128) // 8) == (row % CH))
    ).astype(BF16)
    first = jnp.dot(first_ref[...], spread, preferred_element_type=F32)
    second = jnp.dot(second_ref[...], spread, preferred_element_type=F32).astype(BF16)

    lane = lax.broadcasted_iota(jnp.int32, (48, 256), 1)
    here = lax.broadcasted_iota(jnp.int32, (48, 256), 0) - 16
    out_y = (lane // 128) * 8 + lane % 8
    for tap in range(9):
        total = jnp.zeros((48, 256), F32)
        for k in range(3):
            value = first[tap : tap + 1, 256 * k : 256 * (k + 1)]
            total = total + jnp.where(here == out_y + (k - 1), value, 0.0)
        g_ref[tap] = total.astype(BF16)

    r = lax.broadcasted_iota(jnp.int32, (512, CH), 0)
    c = lax.broadcasted_iota(jnp.int32, (512, CH), 1)
    pick = (((r % 128) // 8) == c).astype(BF16)
    lane = lax.broadcasted_iota(jnp.int32, (512, 256), 1)
    r = lax.broadcasted_iota(jnp.int32, (512, 256), 0)
    shift = (r // 128 - 1) * 8 + r % 8 - ((lane // 128) * 8 + lane % 8)
    for tap in range(9):
        rows = jnp.dot(
            pick, second[CH * tap : CH * (tap + 1)], preferred_element_type=F32
        )
        total = jnp.zeros((512, 256), F32)
        for k in range(3):
            total = total + jnp.where(
                shift == k - 1, rows[:, 256 * k : 256 * (k + 1)], 0.0
            )
        w2_ref[tap] = total.astype(BF16)


def second_convolution(maps_even, maps_odd, w2_ref, second):
    def second_step(p, carry):
        lanes = pl.ds(pl.multiple_of(256 * p, 256), 512)
        acc = jnp.zeros((512, 256), F32)
        for dx in range(3):
            for dz in range(3):
                if dz == 1:
                    source = maps_odd[dx : dx + 8, :, lanes]
                else:
                    source = maps_even[dx : dx + 8, 8 * dz : 8 * dz + 64, lanes]
                acc = acc + jnp.dot(
                    source.reshape(512, 512), w2_ref[3 * dx + dz], preferred_element_type=F32
                )
        out = silu(acc)
        both = jnp.concatenate(
            [out[:, :BLK].reshape(64, 8, BLK), out[:, BLK:].reshape(64, 8, BLK)], axis=1
        )
        second[:, pl.ds(pl.multiple_of(16 * p, 16), 16), :] = both.astype(BF16)
        return carry

    lax.fori_loop(0, PAIRS, second_step, 0)


def encode_kernel(
    place_ref,
    volume_ref,
    left_ref,
    right_ref,
    g_ref,
    w2_ref,
    time_ref,
    space_ref,
    along_y_ref,
    patch_hbm,
    tokens_ref,
    normed_ref,
    second,
    maps_even,
    maps_odd,
    cells,
    planes,
    taps,
    w1,
    patch,
    patch_sem,
):
    copies = [
        pltpu.make_async_copy(
            patch_hbm.at[:, pl.ds(8 * i, 8)],
            patch.at[:, pl.ds(8 * i, 8)],
            patch_sem.at[i],
        )
        for i in range(8)
    ]
    for copy in copies:
        copy.start()
    place = place_ref[0]
    count = place_ref[1]

    cells[:, 0:2] = left_ref[...].astype(F32)
    cells[:, 2:10] = volume_ref[...].astype(F32)
    cells[:, 10:12] = right_ref[...].astype(F32)
    planes[...] = jnp.zeros_like(planes)
    for x in range(XV):
        for f in range(4):
            planes[x, pl.ds(16 + 2 * f, 10, stride=8), :] = cells[f, x, pl.ds(0, 10), :]
            planes[x, pl.ds(2 * f + 1, 10, stride=8), :] = cells[f, x, pl.ds(6, 10), :]
    for dx in range(3):
        for dz in range(3):
            tap = 3 * dx + dz
            for x in range(XM):
                taps[x, :, BLK * tap : BLK * (tap + 1)] = planes[
                    x + dx, 8 * dz : 8 * dz + 80, :
                ].astype(BF16)

    w1[...] = jnp.zeros_like(w1)
    maps_even[:, :, 0:BLK] = jnp.zeros((XM, 80, BLK), BF16)
    maps_even[:, :, 17 * BLK :] = jnp.zeros((XM, 80, BLK), BF16)
    maps_odd[:, :, 0:BLK] = jnp.zeros((XM, 64, BLK), BF16)
    maps_odd[:, :, 17 * BLK :] = jnp.zeros((XM, 64, BLK), BF16)

    x = lax.broadcasted_iota(jnp.int32, (XM, 80, 1), 0) + 8 * place - 1
    r = lax.broadcasted_iota(jnp.int32, (XM, 80, 1), 1)
    z = 8 * (r % 2) + r // 8 - 1
    inside = (x >= 0) & (x < 8 * count) & (z >= 0) & (z < 16)

    def first_step(n, carry):
        before = pl.ds(pl.multiple_of(16 * jnp.maximum(n - 1, 0), 16), 16)
        now = pl.ds(pl.multiple_of(16 * n, 16), 48)
        for tap in range(9):
            w1[tap, before, :] = jnp.zeros((16, 256), BF16)
            w1[tap, now, :] = g_ref[tap]
        acc = jnp.dot(
            taps[...].reshape(XM * 80, 9 * BLK),
            jnp.concatenate([w1[tap, 16:144, :] for tap in range(9)], axis=0),
            preferred_element_type=F32,
        )
        out = jnp.where(inside, silu(acc).reshape(XM, 80, 256), 0.0)
        lanes = pl.ds(pl.multiple_of(256 * n + BLK, BLK), 256)
        maps_even[:, :, lanes] = out.astype(BF16)
        maps_odd[:, :, lanes] = out[:, 8:72].astype(BF16)
        return carry

    lax.fori_loop(0, PAIRS, first_step, 0)

    second_convolution(maps_even, maps_odd, w2_ref, second)
    encoded = jnp.zeros((128, D), F32)
    for x in range(8):
        copies[x].wait()
        for z in range(0, 8, 2):
            i = 8 * x + z
            lhs = jnp.concatenate([second[i], second[i + 1]], axis=1)
            rhs = jnp.concatenate(
                [patch[:, i].reshape(BLK, D), patch[:, i + 1].reshape(BLK, D)], axis=0
            )
            encoded = encoded + jnp.dot(lhs, rhs, preferred_element_type=F32)

    encoded = encoded.reshape(16, 8, D) + time_ref[...][None]
    space = space_ref[...][None] + along_y_ref[...][:, None, :]
    tokens = (encoded + space).reshape(128, D).astype(BF16)
    tokens_ref[...] = tokens
    wide = tokens.astype(F32)
    scale = lax.rsqrt(jnp.mean(wide * wide, axis=-1, keepdims=True) + 1e-05)
    normed_ref[...] = (wide * scale).astype(BF16)


def plane_kernel(at_ref, own_ref, one_ref, three_ref, two_ref, plane_ref):
    spot = jnp.where(at_ref[3] == 0, at_ref[2], at_ref[0])
    for i, ref in enumerate((own_ref, one_ref, two_ref, three_ref)):
        plane_ref[pl.ds((spot + 4 - i) % 4, 1)] = ref[...][None]


def attend_kernel(
    place_ref,
    at_ref,
    tokens_ref,
    n0_ref,
    n1_ref,
    n2_ref,
    n3_ref,
    projector_ref,
    *rest,
):
    parts = rest[:8]
    out_ref, wide, mixing, sems, normed, query, keys, attended = rest[8:]

    def copies(core):
        out = []
        for i, part in enumerate(parts):
            owner = core if i < 4 else 1 - core
            spot = (at_ref[2 * owner] + 4 - i % 4) % 4
            for high in range(2):
                for j, weight in enumerate((wide, mixing)):
                    if owner == 0:
                        end = weight.at[spot, high, :, owner]
                    else:
                        end = weight.at[:, high, spot, owner]
                    start = part.at[:, high, 0:6] if j == 0 else part.at[:, high, 6:8]
                    out.append(
                        pltpu.make_async_copy(start, end, sems.at[4 * i + 2 * high + j])
                    )
        return out

    for core in range(2):

        @pl.when(at_ref[3] == core)
        def _():
            for copy in copies(core):
                copy.start()

    place = place_ref[0]
    contract = (((1,), (1,)), ((), ()))
    for i, ref in enumerate((n0_ref, n1_ref, n2_ref, n3_ref)):
        normed[128 * i : 128 * (i + 1)] = ref[...]
    for core in range(2):

        @pl.when(at_ref[3] == core)
        def _():
            for copy in copies(core):
                copy.wait()

    columns = wide.reshape(384, 8, D)
    query[...] = lax.dot_general(
        normed[0:128], columns[0:128].reshape(D, D), contract, preferred_element_type=F32
    ).astype(BF16)
    for i in range(4):
        keys[:, 512 * i : 512 * (i + 1)] = lax.dot_general(
            normed[...],
            columns[128 + 64 * i : 128 + 64 * (i + 1)].reshape(512, D),
            contract,
            preferred_element_type=F32,
        ).astype(BF16)
    col = lax.broadcasted_iota(jnp.int32, (128, 512), 1)
    row = lax.broadcasted_iota(jnp.int32, (128, 512), 0)
    source = place ^ (col // 128)
    allowed = 4 * source + (col % 8) // 2 <= 4 * place + (row % 8) // 2
    for h in range(HEADS):
        q = query[:, HD * h : HD * (h + 1)]
        k = keys[:, HD * h : HD * (h + 1)]
        v = keys[:, D + HD * h : D + HD * (h + 1)]
        scores = lax.dot_general(q, k, contract, preferred_element_type=F32) * (
            1.0 / math.sqrt(HD)
        )
        scores = jnp.where(allowed, scores, -1e30)
        shifted = jnp.exp(scores - jnp.max(scores, axis=-1, keepdims=True))
        weights = shifted * (1.0 / jnp.sum(shifted, axis=-1, keepdims=True))
        attended[:, HD * h : HD * (h + 1)] = jnp.dot(
            weights.astype(BF16), v, preferred_element_type=F32
        ).astype(BF16)
    residual = tokens_ref[...].astype(F32) + lax.dot_general(
        attended[...], mixing[...].reshape(D, D), contract, preferred_element_type=F32
    )
    scale = lax.rsqrt(jnp.mean(residual * residual, axis=-1, keepdims=True) + 1e-05)
    final = (residual * scale).astype(BF16)
    out_ref[...] = jnp.dot(final, projector_ref[...], preferred_element_type=F32).astype(
        BF16
    )


def vmem():
    return pl.BlockSpec(memory_space=pltpu.VMEM)


def smem():
    return pl.BlockSpec(memory_space=pltpu.SMEM)


def send(array, where):
    pairs = []
    for x in range(4):
        for y in range(4):
            for z in range(4):
                for c in range(2):
                    ends = []
                    for a, b, d, e in ((x, y, z, c), where(x, y, z, c)):
                        a, b, d = a % 4, b % 4, d % 4
                        ends.append(4 * (8 * a + 4 * (b // 2) + d) + 2 * (b % 2) + e)
                    pairs.append(tuple(ends))
    return lax.ppermute(array, ("tile", "tm"), pairs)


def local(
    volume,
    frame_index,
    tile_offset,
    conv_first,
    conv_second,
    patch_weight,
    attend_weight,
    mixing_weight,
    cube_output_projector,
):
    count = lax.axis_size("tile")
    tile_place = lax.axis_index("tile")
    tm_place = lax.axis_index("tm")
    up = [(i, i + 1) for i in range(count - 1)]
    down = [(i + 1, i) for i in range(count - 1)]
    left = lax.ppermute(volume[:, 6:8], "tile", up)
    right = lax.ppermute(volume[:, 0:2], "tile", down)

    core = tm_place % 2
    at = jnp.stack([tile_place // 8, (tile_place // 4) % 2, tile_place % 4, core])
    at = at.astype(jnp.int32)
    shard = jnp.concatenate(
        [attend_weight.T.reshape(2, 6, 8, D), mixing_weight.T.reshape(2, 2, 8, D)], axis=1
    )
    shard = lax.dynamic_index_in_dim(shard, core, axis=0, keepdims=False)
    other = send(shard, lambda x, y, z, c: (x, 3 - y, z, c))
    high = at[1] == 0
    pair = jnp.stack(
        [jnp.where(high, shard, other), jnp.where(high, other, shard)], axis=0
    )
    line = lambda part, k: send(
        part, lambda x, y, z, c: (x + k * c, y, z + k * (1 - c), c)
    )
    cross = lambda part, k: send(
        part, lambda x, y, z, c: (x + k * (1 - c), y, z + k * c, c)
    )
    swap = lambda part: send(part, lambda x, y, z, c: (x, y, z, 1 - c))
    plane = pl.pallas_call(
        plane_kernel,
        out_shape=jax.ShapeDtypeStruct((4, 2, 8, 8, D), BF16),
        in_specs=[smem()] + [vmem()] * 4,
        out_specs=vmem(),
        name="planes",
        compiler_params=pltpu.CompilerParams(vmem_limit_bytes=8 << 20),
    )(at, pair, line(pair, 1), line(pair, 3), line(pair, 2))
    volume, left, right, plane = lax.optimization_barrier((volume, left, right, plane))
    one, two, three = cross(plane, 1), cross(plane, 2), cross(plane, 3)
    swapped = swap(plane)

    frequency = jnp.exp(-math.log(1000.0) * jnp.arange(D, dtype=F32) / D)
    phase_shift = (jnp.arange(D) % 2).astype(F32) * (math.pi / 2)
    time_emb = jnp.sin(
        jnp.repeat(frame_index.astype(F32), 2)[:, None] * frequency + phase_shift
    )
    spot = lambda axis, place: (tile_offset[axis] + BLOCK_EDGE_UNITS * place).astype(F32)
    along_x = jnp.sin(spot(0, tile_place) * frequency)
    along_z = jnp.sin(spot(1, jnp.arange(8) % 2)[:, None] * frequency + 1.0)
    along_y = jnp.sin(spot(2, jnp.arange(16))[:, None] * frequency + 2.0)

    first = conv_first.transpose(2, 3, 1, 4, 0).reshape(9, 48)
    first = jnp.pad(first, ((0, 7), (0, 0)))
    second = conv_second.transpose(2, 3, 1, 4, 0).reshape(144, 48)
    g, w2 = pl.pallas_call(
        weights_kernel,
        out_shape=(
            jax.ShapeDtypeStruct((9, 48, 256), BF16),
            jax.ShapeDtypeStruct((9, 512, 256), BF16),
        ),
        in_specs=[vmem(), vmem()],
        out_specs=(vmem(), vmem()),
        name="conv_weights",
        compiler_params=pltpu.CompilerParams(vmem_limit_bytes=12 << 20),
    )(first, second)

    tokens, normed = pl.pallas_call(
        encode_kernel,
        out_shape=(
            jax.ShapeDtypeStruct((128, D), BF16),
            jax.ShapeDtypeStruct((128, D), BF16),
        ),
        in_specs=[smem()] + [vmem()] * 8 + [pl.BlockSpec(memory_space=pl.ANY)],
        out_specs=(vmem(), vmem()),
        scratch_shapes=[
            pltpu.VMEM((64, 128, BLK), BF16),
            pltpu.VMEM((XM, 80, 18 * BLK), BF16),
            pltpu.VMEM((XM, 64, 18 * BLK), BF16),
            pltpu.VMEM((4, XV, 16, 128), F32),
            pltpu.VMEM((XV, ZV * ROWS, 128), F32),
            pltpu.VMEM((XM, 80, 9 * BLK), BF16),
            pltpu.VMEM((9, 160, 256), BF16),
            pltpu.VMEM((CH, 64, 8, D), BF16),
            pltpu.SemaphoreType.DMA((8,)),
        ],
        name="encode",
        compiler_params=pltpu.CompilerParams(vmem_limit_bytes=40 << 20),
        cost_estimate=pl.CostEstimate(
            flops=15_000_000_000, transcendentals=3_000_000, bytes_accessed=20_000_000
        ),
    )(
        jnp.stack([tile_place, jnp.int32(count)]).astype(jnp.int32),
        volume,
        left,
        right,
        g,
        w2,
        time_emb,
        along_x[None] + along_z,
        along_y,
        patch_weight.reshape(CH, 64, 8, D),
    )
    normed, one, two, three, swapped = lax.optimization_barrier(
        (normed, one, two, three, swapped)
    )
    parts = [plane, one, two, three, swapped, swap(one), swap(two), swap(three)]
    by_chip = lax.ppermute(normed, "tm", [(0, 2), (2, 0), (1, 3), (3, 1)])
    by_core = lax.ppermute(normed, "tm", [(0, 1), (1, 0), (2, 3), (3, 2)])
    by_both = lax.ppermute(by_chip, "tm", [(0, 1), (1, 0), (2, 3), (3, 2)])

    out = pl.pallas_call(
        attend_kernel,
        out_shape=jax.ShapeDtypeStruct((128, 512), BF16),
        in_specs=[smem()] * 2
        + [vmem()] * 6
        + [pl.BlockSpec(memory_space=pl.ANY)] * len(parts),
        out_specs=vmem(),
        scratch_shapes=[
            pltpu.VMEM((4, 2, 4, 2, 6, 8, D), BF16),
            pltpu.VMEM((4, 2, 4, 2, 2, 8, D), BF16),
            pltpu.SemaphoreType.DMA((4 * len(parts),)),
            pltpu.VMEM((512, D), BF16),
            pltpu.VMEM((128, D), BF16),
            pltpu.VMEM((512, 2 * D), BF16),
            pltpu.VMEM((128, D), BF16),
        ],
        name="attend",
        compiler_params=pltpu.CompilerParams(vmem_limit_bytes=26 << 20),
    )(
        tm_place[None].astype(jnp.int32),
        at,
        tokens,
        normed,
        by_core,
        by_chip,
        by_both,
        cube_output_projector,
        *parts,
    )
    return out.reshape(16, 4, 2, 512).transpose(1, 2, 0, 3)[:, None]


def solution(mesh):
    placed = (
        P("tm", "tile", None, None),
        P("tm"),
        P(),
        P(),
        P(),
        P(),
        P(None, "tile"),
        P(None, "tile"),
        P(),
    )
    return jax.shard_map(
        local,
        mesh=mesh,
        in_specs=placed,
        out_specs=P("tm", "tile", None, None, None),
        check_vma=False,
    )
```

```python
import functools
import math

import jax
import jax.numpy as jnp
from jax import lax
from jax.experimental import pallas as pl
from jax.experimental.pallas import tpu as pltpu
from jax.sharding import PartitionSpec as P

CH = 16
D = 1024
HEADS = 8
HD = 128
BLOCK_EDGE_UNITS = 8

F32 = jnp.float32
BF16 = jnp.bfloat16

ROWS = 8
XV = 12
XM = 10
ZV = 12
ZM = 10
BLK = 128
PAIRS = 8


def silu(v):
    return 0.5 * v * (1.0 + jnp.tanh(0.5 * v))


def weights_kernel(first_ref, second_ref, g_ref, w2_ref):
    col = lax.broadcasted_iota(jnp.int32, (48, 768), 1)
    row = lax.broadcasted_iota(jnp.int32, (48, 768), 0)
    spread = (
        ((col // 256) == (row // CH)) & (((col % 128) // 8) == (row % CH))
    ).astype(BF16)
    first = jnp.dot(first_ref[...], spread, preferred_element_type=F32)
    second = jnp.dot(second_ref[...], spread, preferred_element_type=F32).astype(BF16)

    lane = lax.broadcasted_iota(jnp.int32, (48, 256), 1)
    here = lax.broadcasted_iota(jnp.int32, (48, 256), 0) - 16
    out_y = (lane // 128) * 8 + lane % 8
    for tap in range(9):
        total = jnp.zeros((48, 256), F32)
        for k in range(3):
            value = first[tap : tap + 1, 256 * k : 256 * (k + 1)]
            total = total + jnp.where(here == out_y + (k - 1), value, 0.0)
        g_ref[tap] = total.astype(BF16)

    r = lax.broadcasted_iota(jnp.int32, (512, CH), 0)
    c = lax.broadcasted_iota(jnp.int32, (512, CH), 1)
    pick = (((r % 128) // 8) == c).astype(BF16)
    lane = lax.broadcasted_iota(jnp.int32, (512, 256), 1)
    r = lax.broadcasted_iota(jnp.int32, (512, 256), 0)
    shift = (r // 128 - 1) * 8 + r % 8 - ((lane // 128) * 8 + lane % 8)
    for tap in range(9):
        rows = jnp.dot(
            pick, second[CH * tap : CH * (tap + 1)], preferred_element_type=F32
        )
        total = jnp.zeros((512, 256), F32)
        for k in range(3):
            total = total + jnp.where(
                shift == k - 1, rows[:, 256 * k : 256 * (k + 1)], 0.0
            )
        w2_ref[tap] = total.astype(BF16)


def second_convolution(maps_even, maps_odd, w2_ref, second):
    def second_step(p, carry):
        lanes = pl.ds(pl.multiple_of(256 * p, 256), 512)
        acc = jnp.zeros((512, 256), F32)
        for dx in range(3):
            for dz in range(3):
                if dz == 1:
                    source = maps_odd[dx : dx + 8, :, lanes]
                else:
                    source = maps_even[dx : dx + 8, 8 * dz : 8 * dz + 64, lanes]
                acc = acc + jnp.dot(
                    source.reshape(512, 512), w2_ref[3 * dx + dz], preferred_element_type=F32
                )
        out = silu(acc)
        both = jnp.concatenate(
            [out[:, :BLK].reshape(64, 8, BLK), out[:, BLK:].reshape(64, 8, BLK)], axis=1
        )
        second[:, pl.ds(pl.multiple_of(16 * p, 16), 16), :] = both.astype(BF16)
        return carry

    lax.fori_loop(0, PAIRS, second_step, 0)


def encode_kernel(
    place_ref,
    volume_ref,
    left_ref,
    right_ref,
    g_ref,
    w2_ref,
    time_ref,
    space_ref,
    along_y_ref,
    patch_hbm,
    tokens_ref,
    normed_ref,
    second,
    maps_even,
    maps_odd,
    cells,
    planes,
    taps,
    w1,
    patch,
    patch_sem,
):
    copies = [
        pltpu.make_async_copy(
            patch_hbm.at[:, pl.ds(8 * i, 8)],
            patch.at[:, pl.ds(8 * i, 8)],
            patch_sem.at[i],
        )
        for i in range(8)
    ]
    for copy in copies:
        copy.start()
    place = place_ref[0]
    count = place_ref[1]

    cells[:, 0:2] = left_ref[...].astype(F32)
    cells[:, 2:10] = volume_ref[...].astype(F32)
    cells[:, 10:12] = right_ref[...].astype(F32)
    planes[...] = jnp.zeros_like(planes)
    for x in range(XV):
        for f in range(4):
            planes[x, pl.ds(16 + 2 * f, 10, stride=8), :] = cells[f, x, pl.ds(0, 10), :]
            planes[x, pl.ds(2 * f + 1, 10, stride=8), :] = cells[f, x, pl.ds(6, 10), :]
    for dx in range(3):
        for dz in range(3):
            tap = 3 * dx + dz
            for x in range(XM):
                taps[x, :, BLK * tap : BLK * (tap + 1)] = planes[
                    x + dx, 8 * dz : 8 * dz + 80, :
                ].astype(BF16)

    w1[...] = jnp.zeros_like(w1)
    maps_even[:, :, 0:BLK] = jnp.zeros((XM, 80, BLK), BF16)
    maps_even[:, :, 17 * BLK :] = jnp.zeros((XM, 80, BLK), BF16)
    maps_odd[:, :, 0:BLK] = jnp.zeros((XM, 64, BLK), BF16)
    maps_odd[:, :, 17 * BLK :] = jnp.zeros((XM, 64, BLK), BF16)

    x = lax.broadcasted_iota(jnp.int32, (XM, 80, 1), 0) + 8 * place - 1
    r = lax.broadcasted_iota(jnp.int32, (XM, 80, 1), 1)
    z = 8 * (r % 2) + r // 8 - 1
    inside = (x >= 0) & (x < 8 * count) & (z >= 0) & (z < 16)

    def first_step(n, carry):
        before = pl.ds(pl.multiple_of(16 * jnp.maximum(n - 1, 0), 16), 16)
        now = pl.ds(pl.multiple_of(16 * n, 16), 48)
        for tap in range(9):
            w1[tap, before, :] = jnp.zeros((16, 256), BF16)
            w1[tap, now, :] = g_ref[tap]
        acc = jnp.dot(
            taps[...].reshape(XM * 80, 9 * BLK),
            jnp.concatenate([w1[tap, 16:144, :] for tap in range(9)], axis=0),
            preferred_element_type=F32,
        )
        out = jnp.where(inside, silu(acc).reshape(XM, 80, 256), 0.0)
        lanes = pl.ds(pl.multiple_of(256 * n + BLK, BLK), 256)
        maps_even[:, :, lanes] = out.astype(BF16)
        maps_odd[:, :, lanes] = out[:, 8:72].astype(BF16)
        return carry

    lax.fori_loop(0, PAIRS, first_step, 0)

    second_convolution(maps_even, maps_odd, w2_ref, second)
    encoded = jnp.zeros((128, D), F32)
    for x in range(8):
        copies[x].wait()
        for z in range(0, 8, 2):
            i = 8 * x + z
            lhs = jnp.concatenate([second[i], second[i + 1]], axis=1)
            rhs = jnp.concatenate(
                [patch[:, i].reshape(BLK, D), patch[:, i + 1].reshape(BLK, D)], axis=0
            )
            encoded = encoded + jnp.dot(lhs, rhs, preferred_element_type=F32)

    encoded = encoded.reshape(16, 8, D) + time_ref[...][None]
    space = space_ref[...][None] + along_y_ref[...][:, None, :]
    tokens = (encoded + space).reshape(128, D).astype(BF16)
    tokens_ref[...] = tokens
    wide = tokens.astype(F32)
    scale = lax.rsqrt(jnp.mean(wide * wide, axis=-1, keepdims=True) + 1e-05)
    normed_ref[...] = (wide * scale).astype(BF16)


def plane_kernel(at_ref, own_ref, one_ref, three_ref, two_ref, plane_ref):
    spot = jnp.where(at_ref[3] == 0, at_ref[2], at_ref[0])
    for i, ref in enumerate((own_ref, one_ref, two_ref, three_ref)):
        plane_ref[pl.ds((spot + 4 - i) % 4, 1)] = ref[...][None]


def attend_kernel(
    place_ref,
    at_ref,
    tokens_ref,
    n0_ref,
    n1_ref,
    n2_ref,
    n3_ref,
    projector_ref,
    *rest,
):
    parts = rest[:8]
    out_ref, wide, mixing, sems, normed, query, keys, attended = rest[8:]

    def copies(core):
        out = []
        for i, part in enumerate(parts):
            owner = core if i < 4 else 1 - core
            spot = (at_ref[2 * owner] + 4 - i % 4) % 4
            for high in range(2):
                for j, weight in enumerate((wide, mixing)):
                    if owner == 0:
                        end = weight.at[spot, high, :, owner]
                    else:
                        end = weight.at[:, high, spot, owner]
                    start = part.at[:, high, 0:6] if j == 0 else part.at[:, high, 6:8]
                    out.append(
                        pltpu.make_async_copy(start, end, sems.at[4 * i + 2 * high + j])
                    )
        return out

    for core in range(2):

        @pl.when(at_ref[3] == core)
        def _():
            for copy in copies(core):
                copy.start()

    place = place_ref[0]
    contract = (((1,), (1,)), ((), ()))
    for i, ref in enumerate((n0_ref, n1_ref, n2_ref, n3_ref)):
        normed[128 * i : 128 * (i + 1)] = ref[...]
    for core in range(2):

        @pl.when(at_ref[3] == core)
        def _():
            for copy in copies(core):
                copy.wait()

    columns = wide.reshape(384, 8, D)
    query[...] = lax.dot_general(
        normed[0:128], columns[0:128].reshape(D, D), contract, preferred_element_type=F32
    ).astype(BF16)
    for i in range(4):
        keys[:, 512 * i : 512 * (i + 1)] = lax.dot_general(
            normed[...],
            columns[128 + 64 * i : 128 + 64 * (i + 1)].reshape(512, D),
            contract,
            preferred_element_type=F32,
        ).astype(BF16)
    col = lax.broadcasted_iota(jnp.int32, (128, 512), 1)
    row = lax.broadcasted_iota(jnp.int32, (128, 512), 0)
    source = place ^ (col // 128)
    allowed = 4 * source + (col % 8) // 2 <= 4 * place + (row % 8) // 2
    for h in range(HEADS):
        q = query[:, HD * h : HD * (h + 1)]
        k = keys[:, HD * h : HD * (h + 1)]
        v = keys[:, D + HD * h : D + HD * (h + 1)]
        scores = lax.dot_general(q, k, contract, preferred_element_type=F32) * (
            1.0 / math.sqrt(HD)
        )
        scores = jnp.where(allowed, scores, -1e30)
        shifted = jnp.exp(scores - jnp.max(scores, axis=-1, keepdims=True))
        weights = shifted * (1.0 / jnp.sum(shifted, axis=-1, keepdims=True))
        attended[:, HD * h : HD * (h + 1)] = jnp.dot(
            weights.astype(BF16), v, preferred_element_type=F32
        ).astype(BF16)
    residual = tokens_ref[...].astype(F32) + lax.dot_general(
        attended[...], mixing[...].reshape(D, D), contract, preferred_element_type=F32
    )
    scale = lax.rsqrt(jnp.mean(residual * residual, axis=-1, keepdims=True) + 1e-05)
    final = (residual * scale).astype(BF16)
    out_ref[...] = jnp.dot(final, projector_ref[...], preferred_element_type=F32).astype(
        BF16
    )


def vmem():
    return pl.BlockSpec(memory_space=pltpu.VMEM)


def smem():
    return pl.BlockSpec(memory_space=pltpu.SMEM)


def send(array, where):
    pairs = []
    for x in range(4):
        for y in range(4):
            for z in range(4):
                for c in range(2):
                    ends = []
                    for a, b, d, e in ((x, y, z, c), where(x, y, z, c)):
                        a, b, d = a % 4, b % 4, d % 4
                        ends.append(4 * (8 * a + 4 * (b // 2) + d) + 2 * (b % 2) + e)
                    pairs.append(tuple(ends))
    return lax.ppermute(array, ("tile", "tm"), pairs)


def local(
    volume,
    frame_index,
    tile_offset,
    conv_first,
    conv_second,
    patch_weight,
    attend_weight,
    mixing_weight,
    cube_output_projector,
):
    count = lax.axis_size("tile")
    tile_place = lax.axis_index("tile")
    tm_place = lax.axis_index("tm")
    core = tm_place % 2
    at = jnp.stack([tile_place // 8, (tile_place // 4) % 2, tile_place % 4, core])
    at = at.astype(jnp.int32)
    shard = jnp.concatenate(
        [attend_weight.T.reshape(2, 6, 8, D), mixing_weight.T.reshape(2, 2, 8, D)], axis=1
    )
    shard = lax.dynamic_index_in_dim(shard, core, axis=0, keepdims=False)
    other = send(shard, lambda x, y, z, c: (x, 3 - y, z, c))
    high = at[1] == 0
    pair = jnp.stack(
        [jnp.where(high, shard, other), jnp.where(high, other, shard)], axis=0
    )
    line = lambda part, k: send(
        part, lambda x, y, z, c: (x + k * c, y, z + k * (1 - c), c)
    )
    cross = lambda part, k: send(
        part, lambda x, y, z, c: (x + k * (1 - c), y, z + k * c, c)
    )
    swap = lambda part: send(part, lambda x, y, z, c: (x, y, z, 1 - c))
    steps = [line(pair, k) for k in (1, 3, 2)]
    volume, pair = lax.optimization_barrier((volume, pair))
    up = [(i, i + 1) for i in range(count - 1)]
    down = [(i + 1, i) for i in range(count - 1)]
    left = lax.ppermute(volume[:, 6:8], "tile", up)
    right = lax.ppermute(volume[:, 0:2], "tile", down)
    plane = pl.pallas_call(
        plane_kernel,
        out_shape=jax.ShapeDtypeStruct((4, 2, 8, 8, D), BF16),
        in_specs=[smem()] + [vmem()] * 4,
        out_specs=vmem(),
        name="planes",
        compiler_params=pltpu.CompilerParams(vmem_limit_bytes=8 << 20),
    )(at, pair, *steps)
    volume, left, right, plane = lax.optimization_barrier((volume, left, right, plane))
    one, two, three = cross(plane, 1), cross(plane, 2), cross(plane, 3)
    swapped = swap(plane)

    frequency = jnp.exp(-math.log(1000.0) * jnp.arange(D, dtype=F32) / D)
    phase_shift = (jnp.arange(D) % 2).astype(F32) * (math.pi / 2)
    time_emb = jnp.sin(
        jnp.repeat(frame_index.astype(F32), 2)[:, None] * frequency + phase_shift
    )
    spot = lambda axis, place: (tile_offset[axis] + BLOCK_EDGE_UNITS * place).astype(F32)
    along_x = jnp.sin(spot(0, tile_place) * frequency)
    along_z = jnp.sin(spot(1, jnp.arange(8) % 2)[:, None] * frequency + 1.0)
    along_y = jnp.sin(spot(2, jnp.arange(16))[:, None] * frequency + 2.0)

    first = conv_first.transpose(2, 3, 1, 4, 0).reshape(9, 48)
    first = jnp.pad(first, ((0, 7), (0, 0)))
    second = conv_second.transpose(2, 3, 1, 4, 0).reshape(144, 48)
    g, w2 = pl.pallas_call(
        weights_kernel,
        out_shape=(
            jax.ShapeDtypeStruct((9, 48, 256), BF16),
            jax.ShapeDtypeStruct((9, 512, 256), BF16),
        ),
        in_specs=[vmem(), vmem()],
        out_specs=(vmem(), vmem()),
        name="conv_weights",
        compiler_params=pltpu.CompilerParams(vmem_limit_bytes=12 << 20),
    )(first, second)

    tokens, normed = pl.pallas_call(
        encode_kernel,
        out_shape=(
            jax.ShapeDtypeStruct((128, D), BF16),
            jax.ShapeDtypeStruct((128, D), BF16),
        ),
        in_specs=[smem()] + [vmem()] * 8 + [pl.BlockSpec(memory_space=pl.ANY)],
        out_specs=(vmem(), vmem()),
        scratch_shapes=[
            pltpu.VMEM((64, 128, BLK), BF16),
            pltpu.VMEM((XM, 80, 18 * BLK), BF16),
            pltpu.VMEM((XM, 64, 18 * BLK), BF16),
            pltpu.VMEM((4, XV, 16, 128), F32),
            pltpu.VMEM((XV, ZV * ROWS, 128), F32),
            pltpu.VMEM((XM, 80, 9 * BLK), BF16),
            pltpu.VMEM((9, 160, 256), BF16),
            pltpu.VMEM((CH, 64, 8, D), BF16),
            pltpu.SemaphoreType.DMA((8,)),
        ],
        name="encode",
        compiler_params=pltpu.CompilerParams(vmem_limit_bytes=40 << 20),
        cost_estimate=pl.CostEstimate(
            flops=15_000_000_000, transcendentals=3_000_000, bytes_accessed=20_000_000
        ),
    )(
        jnp.stack([tile_place, jnp.int32(count)]).astype(jnp.int32),
        volume,
        left,
        right,
        g,
        w2,
        time_emb,
        along_x[None] + along_z,
        along_y,
        patch_weight.reshape(CH, 64, 8, D),
    )
    normed, one, two, three, swapped = lax.optimization_barrier(
        (normed, one, two, three, swapped)
    )
    parts = [plane, one, two, three, swapped, swap(one), swap(two), swap(three)]
    by_chip = lax.ppermute(normed, "tm", [(0, 2), (2, 0), (1, 3), (3, 1)])
    by_core = lax.ppermute(normed, "tm", [(0, 1), (1, 0), (2, 3), (3, 2)])
    by_both = lax.ppermute(by_chip, "tm", [(0, 1), (1, 0), (2, 3), (3, 2)])

    out = pl.pallas_call(
        attend_kernel,
        out_shape=jax.ShapeDtypeStruct((128, 512), BF16),
        in_specs=[smem()] * 2
        + [vmem()] * 6
        + [pl.BlockSpec(memory_space=pl.ANY)] * len(parts),
        out_specs=vmem(),
        scratch_shapes=[
            pltpu.VMEM((4, 2, 4, 2, 6, 8, D), BF16),
            pltpu.VMEM((4, 2, 4, 2, 2, 8, D), BF16),
            pltpu.SemaphoreType.DMA((4 * len(parts),)),
            pltpu.VMEM((512, D), BF16),
            pltpu.VMEM((128, D), BF16),
            pltpu.VMEM((512, 2 * D), BF16),
            pltpu.VMEM((128, D), BF16),
        ],
        name="attend",
        compiler_params=pltpu.CompilerParams(vmem_limit_bytes=26 << 20),
    )(
        tm_place[None].astype(jnp.int32),
        at,
        tokens,
        normed,
        by_core,
        by_chip,
        by_both,
        cube_output_projector,
        *parts,
    )
    return out.reshape(16, 4, 2, 512).transpose(1, 2, 0, 3)[:, None]


def solution(mesh):
    placed = (
        P("tm", "tile", None, None),
        P("tm"),
        P(),
        P(),
        P(),
        P(),
        P(None, "tile"),
        P(None, "tile"),
        P(),
    )
    return jax.shard_map(
        local,
        mesh=mesh,
        in_specs=placed,
        out_specs=P("tm", "tile", None, None, None),
        check_vma=False,
    )
```

```python
import functools
import math

import jax
import jax.numpy as jnp
from jax import lax
from jax.experimental import pallas as pl
from jax.experimental.pallas import tpu as pltpu
from jax.sharding import PartitionSpec as P

CH = 16
D = 1024
HEADS = 8
HD = 128
BLOCK_EDGE_UNITS = 8

F32 = jnp.float32
BF16 = jnp.bfloat16

ROWS = 8
XV = 12
XM = 10
ZV = 12
ZM = 10
BLK = 128
PAIRS = 8


def silu(v):
    return 0.5 * v * (1.0 + jnp.tanh(0.5 * v))


def weights_kernel(first_ref, second_ref, g_ref, w2_ref):
    col = lax.broadcasted_iota(jnp.int32, (48, 768), 1)
    row = lax.broadcasted_iota(jnp.int32, (48, 768), 0)
    spread = (
        ((col // 256) == (row // CH)) & (((col % 128) // 8) == (row % CH))
    ).astype(BF16)
    first = jnp.dot(first_ref[...], spread, preferred_element_type=F32)
    second = jnp.dot(second_ref[...], spread, preferred_element_type=F32).astype(BF16)

    lane = lax.broadcasted_iota(jnp.int32, (48, 256), 1)
    here = lax.broadcasted_iota(jnp.int32, (48, 256), 0) - 16
    out_y = (lane // 128) * 8 + lane % 8
    for tap in range(9):
        total = jnp.zeros((48, 256), F32)
        for k in range(3):
            value = first[tap : tap + 1, 256 * k : 256 * (k + 1)]
            total = total + jnp.where(here == out_y + (k - 1), value, 0.0)
        g_ref[tap] = total.astype(BF16)

    r = lax.broadcasted_iota(jnp.int32, (512, CH), 0)
    c = lax.broadcasted_iota(jnp.int32, (512, CH), 1)
    pick = (((r % 128) // 8) == c).astype(BF16)
    lane = lax.broadcasted_iota(jnp.int32, (512, 256), 1)
    r = lax.broadcasted_iota(jnp.int32, (512, 256), 0)
    shift = (r // 128 - 1) * 8 + r % 8 - ((lane // 128) * 8 + lane % 8)
    for tap in range(9):
        rows = jnp.dot(
            pick, second[CH * tap : CH * (tap + 1)], preferred_element_type=F32
        )
        total = jnp.zeros((512, 256), F32)
        for k in range(3):
            total = total + jnp.where(
                shift == k - 1, rows[:, 256 * k : 256 * (k + 1)], 0.0
            )
        w2_ref[tap] = total.astype(BF16)


def second_convolution(maps_even, maps_odd, w2_ref, second):
    def second_step(p, carry):
        lanes = pl.ds(pl.multiple_of(256 * p, 256), 512)
        acc = jnp.zeros((512, 256), F32)
        for dx in range(3):
            for dz in range(3):
                if dz == 1:
                    source = maps_odd[dx : dx + 8, :, lanes]
                else:
                    source = maps_even[dx : dx + 8, 8 * dz : 8 * dz + 64, lanes]
                acc = acc + jnp.dot(
                    source.reshape(512, 512), w2_ref[3 * dx + dz], preferred_element_type=F32
                )
        out = silu(acc)
        both = jnp.concatenate(
            [out[:, :BLK].reshape(64, 8, BLK), out[:, BLK:].reshape(64, 8, BLK)], axis=1
        )
        second[:, pl.ds(pl.multiple_of(16 * p, 16), 16), :] = both.astype(BF16)
        return carry

    lax.fori_loop(0, PAIRS, second_step, 0)


def encode_kernel(
    place_ref,
    volume_ref,
    left_ref,
    right_ref,
    g_ref,
    w2_ref,
    time_ref,
    space_ref,
    along_y_ref,
    patch_hbm,
    tokens_ref,
    normed_ref,
    second,
    maps_even,
    maps_odd,
    cells,
    planes,
    taps,
    w1,
    patch,
    patch_sem,
):
    copies = [
        pltpu.make_async_copy(
            patch_hbm.at[:, pl.ds(8 * i, 8)],
            patch.at[:, pl.ds(8 * i, 8)],
            patch_sem.at[i],
        )
        for i in range(8)
    ]
    for copy in copies:
        copy.start()
    place = place_ref[0]
    count = place_ref[1]

    cells[:, 0:2] = left_ref[...].astype(F32)
    cells[:, 2:10] = volume_ref[...].astype(F32)
    cells[:, 10:12] = right_ref[...].astype(F32)
    planes[...] = jnp.zeros_like(planes)
    for x in range(XV):
        for f in range(4):
            planes[x, pl.ds(16 + 2 * f, 10, stride=8), :] = cells[f, x, pl.ds(0, 10), :]
            planes[x, pl.ds(2 * f + 1, 10, stride=8), :] = cells[f, x, pl.ds(6, 10), :]
    for dx in range(3):
        for dz in range(3):
            tap = 3 * dx + dz
            for x in range(XM):
                taps[x, :, BLK * tap : BLK * (tap + 1)] = planes[
                    x + dx, 8 * dz : 8 * dz + 80, :
                ].astype(BF16)

    w1[...] = jnp.zeros_like(w1)
    maps_even[:, :, 0:BLK] = jnp.zeros((XM, 80, BLK), BF16)
    maps_even[:, :, 17 * BLK :] = jnp.zeros((XM, 80, BLK), BF16)
    maps_odd[:, :, 0:BLK] = jnp.zeros((XM, 64, BLK), BF16)
    maps_odd[:, :, 17 * BLK :] = jnp.zeros((XM, 64, BLK), BF16)

    x = lax.broadcasted_iota(jnp.int32, (XM, 80, 1), 0) + 8 * place - 1
    r = lax.broadcasted_iota(jnp.int32, (XM, 80, 1), 1)
    z = 8 * (r % 2) + r // 8 - 1
    inside = (x >= 0) & (x < 8 * count) & (z >= 0) & (z < 16)

    def first_step(n, carry):
        before = pl.ds(pl.multiple_of(16 * jnp.maximum(n - 1, 0), 16), 16)
        now = pl.ds(pl.multiple_of(16 * n, 16), 48)
        for tap in range(9):
            w1[tap, before, :] = jnp.zeros((16, 256), BF16)
            w1[tap, now, :] = g_ref[tap]
        acc = jnp.dot(
            taps[...].reshape(XM * 80, 9 * BLK),
            jnp.concatenate([w1[tap, 16:144, :] for tap in range(9)], axis=0),
            preferred_element_type=F32,
        )
        out = jnp.where(inside, silu(acc).reshape(XM, 80, 256), 0.0)
        lanes = pl.ds(pl.multiple_of(256 * n + BLK, BLK), 256)
        maps_even[:, :, lanes] = out.astype(BF16)
        maps_odd[:, :, lanes] = out[:, 8:72].astype(BF16)
        return carry

    lax.fori_loop(0, PAIRS, first_step, 0)

    second_convolution(maps_even, maps_odd, w2_ref, second)
    encoded = jnp.zeros((128, D), F32)
    for x in range(8):
        copies[x].wait()
        for z in range(0, 8, 2):
            i = 8 * x + z
            lhs = jnp.concatenate([second[i], second[i + 1]], axis=1)
            rhs = jnp.concatenate(
                [patch[:, i].reshape(BLK, D), patch[:, i + 1].reshape(BLK, D)], axis=0
            )
            encoded = encoded + jnp.dot(lhs, rhs, preferred_element_type=F32)

    encoded = encoded.reshape(16, 8, D) + time_ref[...][None]
    space = space_ref[...][None] + along_y_ref[...][:, None, :]
    tokens = (encoded + space).reshape(128, D).astype(BF16)
    tokens_ref[...] = tokens
    wide = tokens.astype(F32)
    scale = lax.rsqrt(jnp.mean(wide * wide, axis=-1, keepdims=True) + 1e-05)
    normed_ref[...] = (wide * scale).astype(BF16)


def plane_kernel(at_ref, own_ref, one_ref, three_ref, two_ref, plane_ref):
    spot = jnp.where(at_ref[3] == 0, at_ref[2], at_ref[0])
    for i, ref in enumerate((own_ref, one_ref, two_ref, three_ref)):
        plane_ref[pl.ds((spot + 4 - i) % 4, 1)] = ref[...][None]


def attend_kernel(
    place_ref,
    at_ref,
    tokens_ref,
    n0_ref,
    n1_ref,
    n2_ref,
    n3_ref,
    projector_ref,
    *rest,
):
    parts = rest[:8]
    out_ref, wide, mixing, sems, normed, query, keys, attended = rest[8:]

    def copies(core):
        out = []
        for i, part in enumerate(parts):
            owner = core if i < 4 else 1 - core
            spot = (at_ref[2 * owner] + 4 - i % 4) % 4
            for high in range(2):
                for j, weight in enumerate((wide, mixing)):
                    if owner == 0:
                        end = weight.at[spot, high, :, owner]
                    else:
                        end = weight.at[:, high, spot, owner]
                    start = part.at[:, high, 0:6] if j == 0 else part.at[:, high, 6:8]
                    out.append(
                        pltpu.make_async_copy(start, end, sems.at[4 * i + 2 * high + j])
                    )
        return out

    for core in range(2):

        @pl.when(at_ref[3] == core)
        def _():
            for copy in copies(core):
                copy.start()

    place = place_ref[0]
    contract = (((1,), (1,)), ((), ()))
    for i, ref in enumerate((n0_ref, n1_ref, n2_ref, n3_ref)):
        normed[128 * i : 128 * (i + 1)] = ref[...]
    for core in range(2):

        @pl.when(at_ref[3] == core)
        def _():
            for copy in copies(core):
                copy.wait()

    columns = wide.reshape(384, 8, D)
    query[...] = lax.dot_general(
        normed[0:128], columns[0:128].reshape(D, D), contract, preferred_element_type=F32
    ).astype(BF16)
    for i in range(4):
        keys[:, 512 * i : 512 * (i + 1)] = lax.dot_general(
            normed[...],
            columns[128 + 64 * i : 128 + 64 * (i + 1)].reshape(512, D),
            contract,
            preferred_element_type=F32,
        ).astype(BF16)
    col = lax.broadcasted_iota(jnp.int32, (128, 512), 1)
    row = lax.broadcasted_iota(jnp.int32, (128, 512), 0)
    source = place ^ (col // 128)
    allowed = 4 * source + (col % 8) // 2 <= 4 * place + (row % 8) // 2
    for h in range(HEADS):
        q = query[:, HD * h : HD * (h + 1)]
        k = keys[:, HD * h : HD * (h + 1)]
        v = keys[:, D + HD * h : D + HD * (h + 1)]
        scores = lax.dot_general(q, k, contract, preferred_element_type=F32) * (
            1.0 / math.sqrt(HD)
        )
        scores = jnp.where(allowed, scores, -1e30)
        shifted = jnp.exp(scores - jnp.max(scores, axis=-1, keepdims=True))
        weights = shifted * (1.0 / jnp.sum(shifted, axis=-1, keepdims=True))
        attended[:, HD * h : HD * (h + 1)] = jnp.dot(
            weights.astype(BF16), v, preferred_element_type=F32
        ).astype(BF16)
    residual = tokens_ref[...].astype(F32) + lax.dot_general(
        attended[...], mixing[...].reshape(D, D), contract, preferred_element_type=F32
    )
    scale = lax.rsqrt(jnp.mean(residual * residual, axis=-1, keepdims=True) + 1e-05)
    final = (residual * scale).astype(BF16)
    out_ref[...] = jnp.dot(final, projector_ref[...], preferred_element_type=F32).astype(
        BF16
    )


def vmem():
    return pl.BlockSpec(memory_space=pltpu.VMEM)


def smem():
    return pl.BlockSpec(memory_space=pltpu.SMEM)


def send(array, where):
    pairs = []
    for x in range(4):
        for y in range(4):
            for z in range(4):
                for c in range(2):
                    ends = []
                    for a, b, d, e in ((x, y, z, c), where(x, y, z, c)):
                        a, b, d = a % 4, b % 4, d % 4
                        ends.append(4 * (8 * a + 4 * (b // 2) + d) + 2 * (b % 2) + e)
                    pairs.append(tuple(ends))
    return lax.ppermute(array, ("tile", "tm"), pairs)


def local(
    volume,
    frame_index,
    tile_offset,
    conv_first,
    conv_second,
    patch_weight,
    attend_weight,
    mixing_weight,
    cube_output_projector,
):
    count = lax.axis_size("tile")
    tile_place = lax.axis_index("tile")
    tm_place = lax.axis_index("tm")
    core = tm_place % 2
    at = jnp.stack([tile_place // 8, (tile_place // 4) % 2, tile_place % 4, core])
    at = at.astype(jnp.int32)
    shard = jnp.concatenate(
        [attend_weight.T.reshape(2, 6, 8, D), mixing_weight.T.reshape(2, 2, 8, D)], axis=1
    )
    shard = lax.dynamic_index_in_dim(shard, core, axis=0, keepdims=False)
    other = send(shard, lambda x, y, z, c: (x, 3 - y, z, c))
    high = at[1] == 0
    pair = jnp.stack(
        [jnp.where(high, shard, other), jnp.where(high, other, shard)], axis=0
    )
    line = lambda part, k: send(
        part, lambda x, y, z, c: (x + k * c, y, z + k * (1 - c), c)
    )
    cross = lambda part, k: send(
        part, lambda x, y, z, c: (x + k * (1 - c), y, z + k * c, c)
    )
    swap = lambda part: send(part, lambda x, y, z, c: (x, y, z, 1 - c))
    steps = [line(pair, k) for k in (1, 3, 2)]
    volume, pair = lax.optimization_barrier((volume, pair))
    up = [(i, i + 1) for i in range(count - 1)]
    down = [(i + 1, i) for i in range(count - 1)]
    left = lax.ppermute(volume[:, 6:8], "tile", up)
    right = lax.ppermute(volume[:, 0:2], "tile", down)
    plane = pl.pallas_call(
        plane_kernel,
        out_shape=jax.ShapeDtypeStruct((4, 2, 8, 8, D), BF16),
        in_specs=[smem()] + [vmem()] * 4,
        out_specs=vmem(),
        name="planes",
        compiler_params=pltpu.CompilerParams(vmem_limit_bytes=8 << 20),
    )(at, pair, *steps)
    volume, left, right, plane = lax.optimization_barrier((volume, left, right, plane))
    one, two, three = cross(plane, 1), cross(plane, 2), cross(plane, 3)
    swapped = swap(plane)

    frequency = jnp.exp(-math.log(1000.0) * jnp.arange(D, dtype=F32) / D)
    phase_shift = (jnp.arange(D) % 2).astype(F32) * (math.pi / 2)
    time_emb = jnp.sin(
        jnp.repeat(frame_index.astype(F32), 2)[:, None] * frequency + phase_shift
    )
    spot = lambda axis, place: (tile_offset[axis] + BLOCK_EDGE_UNITS * place).astype(F32)
    along_x = jnp.sin(spot(0, tile_place) * frequency)
    along_z = jnp.sin(spot(1, jnp.arange(8) % 2)[:, None] * frequency + 1.0)
    along_y = jnp.sin(spot(2, jnp.arange(16))[:, None] * frequency + 2.0)

    first = conv_first.transpose(2, 3, 1, 4, 0).reshape(9, 48)
    first = jnp.pad(first, ((0, 7), (0, 0)))
    second = conv_second.transpose(2, 3, 1, 4, 0).reshape(144, 48)
    g, w2 = pl.pallas_call(
        weights_kernel,
        out_shape=(
            jax.ShapeDtypeStruct((9, 48, 256), BF16),
            jax.ShapeDtypeStruct((9, 512, 256), BF16),
        ),
        in_specs=[vmem(), vmem()],
        out_specs=(vmem(), vmem()),
        name="conv_weights",
        compiler_params=pltpu.CompilerParams(vmem_limit_bytes=12 << 20),
    )(first, second)

    tokens, normed = pl.pallas_call(
        encode_kernel,
        out_shape=(
            jax.ShapeDtypeStruct((128, D), BF16),
            jax.ShapeDtypeStruct((128, D), BF16),
        ),
        in_specs=[smem()] + [vmem()] * 8 + [pl.BlockSpec(memory_space=pl.ANY)],
        out_specs=(vmem(), vmem()),
        scratch_shapes=[
            pltpu.VMEM((64, 128, BLK), BF16),
            pltpu.VMEM((XM, 80, 18 * BLK), BF16),
            pltpu.VMEM((XM, 64, 18 * BLK), BF16),
            pltpu.VMEM((4, XV, 16, 128), F32),
            pltpu.VMEM((XV, ZV * ROWS, 128), F32),
            pltpu.VMEM((XM, 80, 9 * BLK), BF16),
            pltpu.VMEM((9, 160, 256), BF16),
            pltpu.VMEM((CH, 64, 8, D), BF16),
            pltpu.SemaphoreType.DMA((8,)),
        ],
        name="encode",
        compiler_params=pltpu.CompilerParams(vmem_limit_bytes=40 << 20),
        cost_estimate=pl.CostEstimate(
            flops=15_000_000_000, transcendentals=3_000_000, bytes_accessed=20_000_000
        ),
    )(
        jnp.stack([tile_place, jnp.int32(count)]).astype(jnp.int32),
        volume,
        left,
        right,
        g,
        w2,
        time_emb,
        along_x[None] + along_z,
        along_y,
        patch_weight.reshape(CH, 64, 8, D),
    )
    by_chip = lax.ppermute(normed, "tm", [(0, 2), (2, 0), (1, 3), (3, 1)])
    by_core = lax.ppermute(normed, "tm", [(0, 1), (1, 0), (2, 3), (3, 2)])
    by_chip, one, two, three, swapped = lax.optimization_barrier(
        (by_chip, one, two, three, swapped)
    )
    parts = [plane, one, two, three, swapped, swap(one), swap(two), swap(three)]
    by_both = lax.ppermute(by_chip, "tm", [(0, 1), (1, 0), (2, 3), (3, 2)])

    out = pl.pallas_call(
        attend_kernel,
        out_shape=jax.ShapeDtypeStruct((128, 512), BF16),
        in_specs=[smem()] * 2
        + [vmem()] * 6
        + [pl.BlockSpec(memory_space=pl.ANY)] * len(parts),
        out_specs=vmem(),
        scratch_shapes=[
            pltpu.VMEM((4, 2, 4, 2, 6, 8, D), BF16),
            pltpu.VMEM((4, 2, 4, 2, 2, 8, D), BF16),
            pltpu.SemaphoreType.DMA((4 * len(parts),)),
            pltpu.VMEM((512, D), BF16),
            pltpu.VMEM((128, D), BF16),
            pltpu.VMEM((512, 2 * D), BF16),
            pltpu.VMEM((128, D), BF16),
        ],
        name="attend",
        compiler_params=pltpu.CompilerParams(vmem_limit_bytes=26 << 20),
    )(
        tm_place[None].astype(jnp.int32),
        at,
        tokens,
        normed,
        by_core,
        by_chip,
        by_both,
        cube_output_projector,
        *parts,
    )
    return out.reshape(16, 4, 2, 512).transpose(1, 2, 0, 3)[:, None]


def solution(mesh):
    placed = (
        P("tm", "tile", None, None),
        P("tm"),
        P(),
        P(),
        P(),
        P(),
        P(None, "tile"),
        P(None, "tile"),
        P(),
    )
    return jax.shard_map(
        local,
        mesh=mesh,
        in_specs=placed,
        out_specs=P("tm", "tile", None, None, None),
        check_vma=False,
    )
```
